512 devices in a mesh: wide: 32 (over y, x_hi, core), narrow: 8 (over z), act: 2 (over x_lo).
Axes of the slice: x: 4 (x_hi: 2, x_lo: 2; x = x_hi * 2 + x_lo), y: 8, z: 8, core: 2. Of those that a mesh axis runs over, the one named last changes fastest.
Arguments:
- value_now: float32 [64, 64, 128, 128], P('wide', 'narrow'), may hold values from -8 to 8, as said below
- cost_first: float32 [8, 64], replicated, may hold values from -6 to 332, as said below
- cost_second: float32 [8, 64], replicated, may hold values from -6 to 6
- cost_third: float32 [8, 128], replicated, may hold values from -6 to 6
- cost_fourth: float32 [8, 128], replicated, may hold values from -6 to 6
- trans_weights: float32 [8, 4, 65], replicated, may hold values from 0.0001 to 1
- trans_offsets: int32 [8, 4], replicated, may hold values from -32 to 32
- action_order: int32 [8], replicated, may hold values from 0 to 7, each once
Outputs:
- new_value: float32 [64, 64, 128, 128], P('wide', 'narrow')
- choice_prob: bfloat16 [8, 64, 64, 128, 128], P('act', 'wide', 'narrow')
The draws below stay inside these ranges and needn't reach their ends.
Inputs may be any that keep to these rules, and one draw needn't show every extreme that they name: `value_now`: A value function of order one with rough and broad variation. `cost_first`: flow utility terms of order one in most entries.
All inputs are finite; a program needn't handle non-finite values.
Results may differ from the reference program's by a relative error of at most 0.001.
Values sent between devices are 32-bit elements; how exact they have to be, the bound alone decides.
A program may use at most 64 MiB of HBM per device.

```python
import math
import jax
import jax.numpy as jnp
from jax import lax

ACTIONS = 8
HALF = 32
BAND = 65
N2 = 128
N3 = 128
N0 = 64
N1 = 64


def draw_value_now(key, part):
    shape = (N0, N1, N2, N3)
    field = 0.5 * jnp.clip(jax.random.normal(jax.random.fold_in(key, 1), shape, jnp.float32), -6.0, 6.0)
    lengths = (N0, N1, N2, N3)
    for axis_id in range(4):
        amplitude = jax.random.uniform(jax.random.fold_in(key, 10 + axis_id), (), jnp.float32, 0.5, 1.0)
        frequency = jax.random.randint(jax.random.fold_in(key, 20 + axis_id), (), 1, 4).astype(jnp.float32)
        phase_shift = jax.random.uniform(jax.random.fold_in(key, 30 + axis_id), (), jnp.float32, -math.pi, math.pi)
        coords = jnp.arange(lengths[axis_id], dtype=jnp.float32)
        profile = amplitude * jnp.cos(2.0 * math.pi * frequency * coords / lengths[axis_id] + phase_shift)
        view_shape = [1, 1, 1, 1]
        view_shape[axis_id] = lengths[axis_id]
        field = field + profile.reshape(view_shape)
    return field


def draw_cost_first(key, part):
    drawn = jnp.clip(jax.random.normal(jax.random.fold_in(key, 2), (ACTIONS, N0), jnp.float32), -6.0, 6.0)
    return drawn


def place_ends(array, stream_key, smallest, top_value):
    longest = array.shape.index(max(array.shape))
    spots = []
    for shift in (0, 1):
        where = [jax.random.randint(jax.random.fold_in(stream_key, axis), (), 0, length) for axis, length in enumerate(array.shape)]
        where[longest] = (where[longest] + shift) % array.shape[longest]
        spots.append(tuple(where))
    return array.at[spots[0]].set(smallest).at[spots[1]].set(top_value)


def noise(rng, dims, width, most, held_as=jnp.bfloat16):
    entries = jax.random.normal(rng, dims, jnp.float32) * width
    return jnp.minimum(jnp.maximum(entries, -most), most).astype(held_as)


def setup_inputs(seed: int = 0) -> dict:
    arg_keys = jax.random.split(jax.random.key(seed), 9)
    value_now = draw_value_now(jax.random.fold_in(arg_keys[8], 71), 0)
    cost_first = draw_cost_first(jax.random.fold_in(arg_keys[8], 71), 0)
    cost_second = noise(arg_keys[2], (ACTIONS, N1), 1.0, 6.0, jnp.float32)
    cost_third = noise(arg_keys[3], (ACTIONS, N2), 1.0, 6.0, jnp.float32)
    cost_fourth = noise(arg_keys[4], (ACTIONS, N3), 1.0, 6.0, jnp.float32)
    trans_weights = jnp.clip(jnp.exp(jax.random.uniform(arg_keys[5], (ACTIONS, 4, BAND), jnp.float32, math.log(0.0001), math.log(1.0))), 0.0001, 1.0)
    trans_offsets = place_ends(jax.random.randint(arg_keys[6], (ACTIONS, 4), -HALF, HALF + 1), jax.random.fold_in(arg_keys[6], 1), -HALF, HALF).astype(jnp.int32)
    action_order = jax.random.permutation(arg_keys[7], ACTIONS).astype(jnp.int32)
    return {"value_now": value_now, "cost_first": cost_first, "cost_second": cost_second, "cost_third": cost_third, "cost_fourth": cost_fourth, "trans_weights": trans_weights, "trans_offsets": trans_offsets, "action_order": action_order}


DISCOUNT = 0.95
HIGHEST = lax.Precision.HIGHEST


def transition(weights, offset, length):
    band_len = weights.shape[0]
    half_band = (band_len - 1) // 2
    normed = weights / jnp.sum(weights)
    row_ids = jnp.arange(length, dtype=jnp.int32)
    tap_ids = jnp.arange(band_len, dtype=jnp.int32)
    target = jnp.clip(row_ids[:, None] + offset + tap_ids[None, :] - half_band, 0, length - 1)
    matched = (target[:, :, None] == row_ids[None, None, :]).astype(normed.dtype)
    return jnp.einsum("ijk,j->ik", matched, normed, precision=HIGHEST)


def expect(value_now, weights, offsets):
    lengths = value_now.shape
    field = value_now
    for axis_id in range(4):
        matrix = transition(weights[axis_id], offsets[axis_id], lengths[axis_id])
        field = jnp.moveaxis(jnp.tensordot(matrix, field, axes=([1], [axis_id]), precision=HIGHEST), 0, axis_id)
    return field


def reference(value_now, cost_first, cost_second, cost_third, cost_fourth, trans_weights, trans_offsets, action_order):
    def one_action(action_id):
        expected = expect(value_now, trans_weights[action_id], trans_offsets[action_id])
        utility = (cost_first[action_id][:, None, None, None] + cost_second[action_id][None, :, None, None]
                   + cost_third[action_id][None, None, :, None] + cost_fourth[action_id][None, None, None, :])
        return utility + DISCOUNT * expected

    scores = lax.map(one_action, jnp.arange(ACTIONS, dtype=jnp.int32))
    top_score = jnp.max(scores, axis=0)
    total = jnp.sum(jnp.exp(scores - top_score), axis=0)
    new_value = top_score + jnp.log(total)

    def one_prob(action_id):
        return jnp.exp(scores[action_id] - new_value).astype(jnp.bfloat16)

    choice_prob = lax.map(one_prob, action_order)
    return new_value, choice_prob
```

```python
import jax
import jax.numpy as jnp
from jax import lax
from jax.experimental import pallas as pl
from jax.experimental.pallas import tpu as pltpu
from jax.sharding import PartitionSpec as P

DISCOUNT = 0.95
MESH = pl.DeviceIdType.MESH
F32 = jnp.float32
BF16 = jnp.bfloat16
VMEM = pl.BlockSpec(memory_space=pltpu.VMEM)
SMEM = pl.BlockSpec(memory_space=pltpu.SMEM)
LIMIT = 56 * 1024 * 1024


def place():
    wide = lax.axis_index("wide")
    return lax.div(wide, 4), lax.rem(wide, 4), lax.axis_index("narrow"), lax.axis_index("act")


def partner(step, t, q):
    return lax.rem(t + lax.div(step, 4), 8), lax.rem(q + lax.rem(step, 4), 4)


def halves(x):
    high = x.astype(BF16)
    low = (x - high.astype(F32)).astype(BF16)
    return high, low


def build_kernel(order_ref, offs_ref, w_ref, c0_ref, c1_ref, w2_ref, w3_ref):
    act = lax.axis_index("act")

    def toeplitz(a, d, length):
        row = w_ref[pl.ds(a, 1), d, :]
        row = row / jnp.sum(row)
        shift = lax.rem(offs_ref[a, d] - 32 + 256, 256)
        spread = jnp.broadcast_to(pltpu.roll(jnp.broadcast_to(row, (8, 256)), shift, 1)[0:1], (length, 256))
        number = lax.broadcasted_iota(jnp.int32, (length, 256), 0)
        lane = lax.broadcasted_iota(jnp.int32, (length, 256), 1)
        bit = 1
        while bit < length:
            spread = jnp.where(lax.rem(lax.div(number, bit), 2) == 1, pltpu.roll(spread, bit, 1), spread)
            bit *= 2
        zero = jnp.zeros_like(spread)
        below = jnp.sum(jnp.where(lane >= 192, spread, zero), axis=1, keepdims=True)
        above = jnp.sum(jnp.where((lane >= length) & (lane < 192), spread, zero), axis=1, keepdims=True)
        full = jnp.where(lane == 0, spread + below, jnp.where(lane == length - 1, spread + above, spread))
        full = jnp.where(lane < length, full, zero)
        high = full.astype(BF16).astype(F32)
        return high, full - high

    def one(j, carry):
        a = order_ref[j]
        for d, ref in ((0, c0_ref), (1, c1_ref)):
            high, low = toeplitz(a, d, 64)
            both = high + pltpu.roll(high, 64, 1) + pltpu.roll(low, 128, 1)
            ref[0, j] = both[:, :128]
            ref[1, j] = both[:, 128:]
        return carry

    lax.fori_loop(0, 8, one, 0)

    def mine(j, carry):
        a = order_ref[act * 4 + j]
        for d, ref in ((2, w2_ref), (3, w3_ref)):
            high, low = toeplitz(a, d, 128)
            ref[j, :, 0:128] = high[:, :128].astype(BF16)
            ref[j, :, 128:256] = high[:, :128].astype(BF16)
            ref[j, :, 256:384] = low[:, :128].astype(BF16)
        return carry

    lax.fori_loop(0, 4, mine, 0)


def build(order, offsets, weights):
    padded = jnp.pad(weights, ((0, 0), (0, 0), (0, 256 - weights.shape[2])))
    return pl.pallas_call(
        build_kernel,
        out_shape=(
            jax.ShapeDtypeStruct((2, 8, 64, 128), F32),
            jax.ShapeDtypeStruct((2, 8, 64, 128), F32),
            jax.ShapeDtypeStruct((4, 128, 384), BF16),
            jax.ShapeDtypeStruct((4, 128, 384), BF16),
        ),
        in_specs=[SMEM, SMEM, VMEM],
        out_specs=(VMEM,) * 4,
        name="build",
    )(order, offsets, padded)


def spread_kernel(vt_ref, ga_ref, gb_ref, send_sem, recv_sem, local_sem, ring_send, ring_recv):
    y, q, z, act = place()
    wide = 4 * y + q
    barrier = pltpu.get_barrier_semaphore()

    def at_a(step):
        t, p = partner(step, y, q)
        return t * 8 + p * 2 + act, {"wide": 4 * t + p, "narrow": z, "act": act}

    def at_b(step):
        t, p = partner(step, z, q)
        return 64 + t * 8 + p * 2 + act, {"wide": 4 * y + p, "narrow": t, "act": act}

    def greet(step, carry):
        pl.semaphore_signal(barrier, inc=1, device_id=at_a(step)[1], device_id_type=MESH)
        pl.semaphore_signal(barrier, inc=1, device_id=at_b(step)[1], device_id_type=MESH)
        return carry

    lax.fori_loop(1, 32, greet, 0)
    own = [
        pltpu.make_async_copy(vt_ref.at[y * 8 + q * 2 + act], ga_ref.at[z, wide], local_sem.at[0]),
        pltpu.make_async_copy(vt_ref.at[64 + z * 8 + q * 2 + act], gb_ref.at[y, 4 * z + q], local_sem.at[1]),
    ]
    for copy in own:
        copy.start()
    pl.semaphore_wait(barrier, 62)

    def send(step, carry):
        row, device = at_a(step)
        pltpu.make_async_remote_copy(
            vt_ref.at[row], ga_ref.at[z, wide], send_sem.at[0], recv_sem.at[0], device, MESH
        ).start()
        row, device = at_b(step)
        pltpu.make_async_remote_copy(
            vt_ref.at[row], gb_ref.at[y, 4 * z + q], send_sem.at[1], recv_sem.at[1], device, MESH
        ).start()
        return carry

    lax.fori_loop(1, 32, send, 0)
    for copy in own:
        copy.wait()
    streams = (
        (ga_ref, z, lambda t: {"wide": wide, "narrow": t, "act": act}),
        (gb_ref, y, lambda t: {"wide": 4 * t + q, "narrow": z, "act": act}),
    )
    for index, (ref, _, _) in enumerate(streams):
        part = ref.at[0, pl.ds(0, 31)]
        pltpu.make_async_copy(part, part, recv_sem.at[index]).wait()

    def hop(index, step, half, way):
        ref, t, device = streams[index]
        block = lax.rem(t + 8 - way * (step - 1), 8)
        piece = ref.at[block, pl.ds(16 * half, 16)]
        side = 0 if way > 0 else 1
        return pltpu.make_async_remote_copy(
            piece,
            piece,
            ring_send.at[index, step - 1, half, side],
            ring_recv.at[index, step - 1, half, side],
            device(lax.rem(t + 8 + way, 8)),
            MESH,
        )

    started = []
    for step in (1, 2, 3, 4):
        for half in (0, 1):
            for index in (0, 1):
                for way in (1, -1):
                    if step > 1 and not (step == 4 and half != (0 if way > 0 else 1)):
                        hop(index, step - 1, half, way).wait_recv()
                    if step == 4 and half != (0 if way > 0 else 1):
                        continue
                    copy = hop(index, step, half, way)
                    copy.start()
                    started.append(copy)
    for index in (0, 1):
        hop(index, 3, 1, 1).wait_recv()
        hop(index, 3, 0, -1).wait_recv()
        hop(index, 4, 0, 1).wait_recv()
        hop(index, 4, 1, -1).wait_recv()
    for copy in started:
        copy.wait_send()
    for index, (ref, _, _) in enumerate(streams):
        part = ref.at[0, pl.ds(0, 31)]
        pltpu.make_async_copy(part, part, send_sem.at[index]).wait()


def spread(vt):
    return pl.pallas_call(
        spread_kernel,
        out_shape=(jax.ShapeDtypeStruct((8, 32, 16, 128), F32),) * 2,
        in_specs=[VMEM],
        out_specs=(VMEM, VMEM),
        scratch_shapes=[
            pltpu.SemaphoreType.DMA((2,)),
            pltpu.SemaphoreType.DMA((2,)),
            pltpu.SemaphoreType.DMA((2,)),
            pltpu.SemaphoreType.DMA((2, 4, 2, 2)),
            pltpu.SemaphoreType.DMA((2, 4, 2, 2)),
        ],
        compiler_params=pltpu.CompilerParams(collective_id=0, has_side_effects=True, vmem_limit_bytes=LIMIT),
        name="spread",
    )(vt)


def stack(x):
    high, low = halves(x)
    return jnp.concatenate([high, low, high, high], axis=0)


def outer_kernel(c0_ref, c1_ref, ga_ref, gb_ref, ea_ref, eb_ref, za_ref, zb_ref):
    y, q, z, act = place()

    def wide_rows(ref, *index):
        return jnp.concatenate([ref[(half,) + index] for half in (0, 1)], axis=-1)

    def own_rows(ref, t):
        return wide_rows(ref, slice(None), pl.ds(t * 8, 8)).reshape(64, 256).astype(BF16)

    mine1 = own_rows(c1_ref, z)
    mine0 = own_rows(c0_ref, y)

    def first_a(w, carry):
        left = ga_ref[:, w, 0:8, :].reshape(64, 128)
        right = ga_ref[:, w, 8:16, :].reshape(64, 128)
        out = jnp.dot(mine1, stack(jnp.concatenate([left, right], axis=1)), preferred_element_type=F32)
        za_ref[:, pl.ds(16 * w, 8), :] = out[:, :128].reshape(8, 8, 128)
        za_ref[:, pl.ds(16 * w + 8, 8), :] = out[:, 128:].reshape(8, 8, 128)
        return carry

    lax.fori_loop(0, 32, first_a, 0, unroll=4)

    def second_a(a, carry):
        left = jnp.concatenate([wide_rows(c0_ref, a, pl.ds(half, 32, stride=2)) for half in (0, 1)], axis=0)
        left = left.astype(BF16)
        for i in range(0, 8, 2):
            right = jnp.concatenate(
                [za_ref[a, pl.ds(i, 64, stride=8), :], za_ref[a, pl.ds(i + 1, 64, stride=8), :]], axis=1
            )
            out = jnp.dot(left, stack(right), preferred_element_type=F32)
            for k in range(2):
                for half in range(2):
                    ea_ref[pl.ds(a * 16 + half * 8 + i + k, 32, stride=128), :] = out[
                        32 * half : 32 * half + 32, 128 * k : 128 * k + 128
                    ]
        return carry

    lax.fori_loop(0, 8, second_a, 0)

    def first_b(s, carry):
        for i in range(0, 8, 2):
            left = gb_ref[:, pl.ds(64 * s + i, 8, stride=8), :].reshape(64, 128)
            right = gb_ref[:, pl.ds(64 * s + i + 1, 8, stride=8), :].reshape(64, 128)
            out = jnp.dot(mine0, stack(jnp.concatenate([left, right], axis=1)), preferred_element_type=F32)
            zb_ref[pl.ds((8 * s + i) * 64, 64), :] = out[:, :128]
            zb_ref[pl.ds((8 * s + i + 1) * 64, 64), :] = out[:, 128:]
        return carry

    lax.fori_loop(0, 8, first_b, 0)

    def second_b(a, carry):
        left = wide_rows(c1_ref, a).astype(BF16)
        for p in range(4):
            right = jnp.concatenate(
                [zb_ref[pl.ds(a * 8 + 2 * p + half, 64, stride=64), :] for half in range(2)], axis=1
            )
            out = jnp.dot(left, stack(right), preferred_element_type=F32)
            for half in range(2):
                eb_ref[:, p, a, pl.ds(half * 8, 8), :] = out[:, 128 * half : 128 * half + 128].reshape(8, 8, 128)
        return carry

    lax.fori_loop(0, 8, second_b, 0)


def outer(c0, c1, ga, gb):
    ea, eb = pl.pallas_call(
        outer_kernel,
        out_shape=(
            jax.ShapeDtypeStruct((4096, 128), F32),
            jax.ShapeDtypeStruct((8, 4, 8, 16, 128), F32),
        ),
        in_specs=[VMEM] * 4,
        out_specs=(VMEM, VMEM),
        scratch_shapes=[pltpu.VMEM((8, 512, 128), F32), pltpu.VMEM((4096, 128), F32)],
        compiler_params=pltpu.CompilerParams(vmem_limit_bytes=LIMIT),
        name="outer",
    )(c0, c1, ga, gb.reshape(8, 512, 128))
    return ea.reshape(32, 2, 64, 128), eb.reshape(8, 4, 2, 64, 128)


def home_kernel(ea_ref, eb_ref, r_ref, send_sem, recv_sem, local_sem):
    y, q, z, act = place()
    wide = 4 * y + q
    row_a = y * 8 + q * 2 + act
    row_b = 64 + z * 8 + q * 2 + act
    barrier = pltpu.get_barrier_semaphore()

    def at_a(step):
        t, p = partner(lax.div(step, 2), y, q)
        g = lax.rem(act + lax.rem(step, 2), 2)
        return ea_ref.at[4 * t + p, g], {"wide": 4 * t + p, "narrow": z, "act": g}

    def at_b(step):
        t, p = partner(lax.div(step, 2), z, q)
        g = lax.rem(act + lax.rem(step, 2), 2)
        return eb_ref.at[t, p, g], {"wide": 4 * y + p, "narrow": t, "act": g}

    def greet(step, carry):
        pl.semaphore_signal(barrier, inc=1, device_id=at_a(step)[1], device_id_type=MESH)
        pl.semaphore_signal(barrier, inc=1, device_id=at_b(step)[1], device_id_type=MESH)
        return carry

    lax.fori_loop(1, 64, greet, 0)
    own = [
        pltpu.make_async_copy(ea_ref.at[wide, act], r_ref.at[row_a], local_sem.at[0]),
        pltpu.make_async_copy(eb_ref.at[z, q, act], r_ref.at[row_b], local_sem.at[1]),
    ]
    for copy in own:
        copy.start()
    pl.semaphore_wait(barrier, 126)

    def send(step, carry):
        src, device = at_a(step)
        pltpu.make_async_remote_copy(
            src, r_ref.at[row_a], send_sem.at[0], recv_sem.at[0], device, MESH
        ).start()
        src, device = at_b(step)
        pltpu.make_async_remote_copy(
            src, r_ref.at[row_b], send_sem.at[1], recv_sem.at[1], device, MESH
        ).start()
        return carry

    lax.fori_loop(1, 64, send, 0)
    for copy in own:
        copy.wait()
    for index in (0, 1):
        part = r_ref.at[pl.ds(0, 63)]
        pltpu.make_async_copy(part, part, recv_sem.at[index]).wait()
        pltpu.make_async_copy(part, part, send_sem.at[index]).wait()


def home(ea, eb):
    return pl.pallas_call(
        home_kernel,
        out_shape=jax.ShapeDtypeStruct((128, 64, 128), F32),
        in_specs=[VMEM, VMEM],
        out_specs=VMEM,
        scratch_shapes=[pltpu.SemaphoreType.DMA((2,))] * 3,
        compiler_params=pltpu.CompilerParams(collective_id=1, has_side_effects=True, vmem_limit_bytes=LIMIT),
        name="home",
    )(ea, eb)


def inner_kernel(u_ref, third_ref, fourth_ref, w2_ref, w3_ref, r_ref, score_ref, lse_ref):
    def one(j, carry):
        scores = []
        for a in range(4):
            rows = r_ref[pl.ds(a * 16 + j, 128, stride=64), :]
            high, low = halves(rows)
            mid = jnp.dot(
                w2_ref[a], jnp.concatenate([high, low, high], axis=0), preferred_element_type=F32
            )
            high, low = halves(mid)
            expected = lax.dot_general(
                jnp.concatenate([high, low, high], axis=1),
                w3_ref[a],
                (((1,), (1,)), ((), ())),
                preferred_element_type=F32,
            )
            util = (u_ref[a, j] + third_ref[:, a : a + 1]) + fourth_ref[a : a + 1, :]
            score = util + DISCOUNT * expected
            score_ref[a, j] = score
            scores.append(score)
        top = jnp.maximum(jnp.maximum(scores[0], scores[1]), jnp.maximum(scores[2], scores[3]))
        total = sum(jnp.exp(s - top) for s in scores)
        lse_ref[j] = top + jnp.log(total)
        return carry

    lax.fori_loop(0, 16, one, 0)


def inner(u, third, fourth, w2, w3, r):
    return pl.pallas_call(
        inner_kernel,
        out_shape=(
            jax.ShapeDtypeStruct((4, 16, 128, 128), F32),
            jax.ShapeDtypeStruct((16, 128, 128), F32),
        ),
        in_specs=[SMEM] + [VMEM] * 5,
        out_specs=(VMEM, VMEM),
        compiler_params=pltpu.CompilerParams(vmem_limit_bytes=LIMIT),
        name="inner",
    )(u, third, fourth, w2, w3, r.reshape(8192, 128))


def body(
    value_now,
    cost_first,
    cost_second,
    cost_third,
    cost_fourth,
    trans_weights,
    trans_offsets,
    action_order,
):
    act = lax.axis_index("act")
    mine = lax.dynamic_slice_in_dim(action_order, act * 4, 4)
    start_first = lax.axis_index("wide") * 2
    start_second = lax.axis_index("narrow") * 8
    util_first = lax.dynamic_slice_in_dim(jnp.take(cost_first, mine, axis=0), start_first, 2, 1)
    util_second = lax.dynamic_slice_in_dim(jnp.take(cost_second, mine, axis=0), start_second, 8, 1)
    u = (util_first[:, :, None] + util_second[:, None, :]).reshape(4, 16)
    third = jnp.take(cost_third, mine, axis=0).T
    fourth = jnp.take(cost_fourth, mine, axis=0)

    c0, c1, w2, w3 = build(action_order, trans_offsets, trans_weights)
    vt = value_now.transpose(2, 0, 1, 3).reshape(128, 16, 128)
    ga, gb = spread(vt)
    ea, eb = outer(c0, c1, ga, gb)
    r = home(ea, eb)
    scores, lse = inner(u, third, fourth, w2, w3, r)
    other = lax.ppermute(lse, "act", [(0, 1), (1, 0)])
    top = jnp.maximum(lse, other)
    new_value = top + jnp.log(jnp.exp(lse - top) + jnp.exp(other - top))
    choice_prob = jnp.exp(scores - new_value).astype(BF16)
    return new_value.reshape(2, 8, 128, 128), choice_prob.reshape(4, 2, 8, 128, 128)


def solution(mesh):
    return jax.shard_map(
        body,
        mesh=mesh,
        in_specs=(P("wide", "narrow", None, None), P(), P(), P(), P(), P(), P(), P()),
        out_specs=(P("wide", "narrow", None, None), P("act", "wide", "narrow", None, None)),
        check_vma=False,
    )
```

```python
import jax
import jax.numpy as jnp
from jax import lax
from jax.experimental import pallas as pl
from jax.experimental.pallas import tpu as pltpu
from jax.sharding import PartitionSpec as P

DISCOUNT = 0.95
MESH = pl.DeviceIdType.MESH
F32 = jnp.float32
BF16 = jnp.bfloat16
VMEM = pl.BlockSpec(memory_space=pltpu.VMEM)
SMEM = pl.BlockSpec(memory_space=pltpu.SMEM)
LIMIT = 56 * 1024 * 1024


def place():
    wide = lax.axis_index("wide")
    return lax.div(wide, 4), lax.rem(wide, 4), lax.axis_index("narrow"), lax.axis_index("act")


def partner(step, t, q):
    return lax.rem(t + lax.div(step, 4), 8), lax.rem(q + lax.rem(step, 4), 4)


def halves(x):
    high = x.astype(BF16)
    low = (x - high.astype(F32)).astype(BF16)
    return high, low


def build_kernel(
    order_ref, offs_ref, first_ref, second_ref, w_ref, third_ref, fourth_ref,
    c0_ref, c1_ref, w2_ref, w3_ref, u_ref, column_ref, row_ref, pad_ref,
):
    act = lax.axis_index("act")
    first_row = lax.axis_index("wide") * 2
    second_row = lax.axis_index("narrow") * 8
    pad_ref[...] = jnp.zeros_like(pad_ref)
    pad_ref[:, :, 0:65] = w_ref[...]

    def toeplitz(a, d, length):
        row = pad_ref[pl.ds(a, 1), d, :]
        row = row / jnp.sum(row)
        shift = lax.rem(offs_ref[d, a] - 32 + 256, 256)
        spread = jnp.broadcast_to(pltpu.roll(jnp.broadcast_to(row, (8, 256)), shift, 1)[0:1], (length, 256))
        number = lax.broadcasted_iota(jnp.int32, (length, 256), 0)
        lane = lax.broadcasted_iota(jnp.int32, (length, 256), 1)
        bit = 1
        while bit < length:
            spread = jnp.where((number & bit) != 0, pltpu.roll(spread, bit, 1), spread)
            bit *= 2
        zero = jnp.zeros_like(spread)
        below = jnp.sum(jnp.where(lane >= 192, spread, zero), axis=1, keepdims=True)
        above = jnp.sum(jnp.where((lane >= length) & (lane < 192), spread, zero), axis=1, keepdims=True)
        full = jnp.where(lane == 0, spread + below, jnp.where(lane == length - 1, spread + above, spread))
        full = jnp.where(lane < length, full, zero)
        high = full.astype(BF16).astype(F32)
        return high, full - high

    def one(j, carry):
        a = order_ref[j]
        for d, ref in ((0, c0_ref), (1, c1_ref)):
            high, low = toeplitz(a, d, 64)
            both = high + pltpu.roll(high, 64, 1) + pltpu.roll(low, 128, 1)
            ref[0, j] = both[:, :128]
            ref[1, j] = both[:, 128:]
        return carry

    lax.fori_loop(0, 8, one, 0)

    def mine(j, carry):
        a = order_ref[act * 4 + j]
        for d, ref in ((2, w2_ref), (3, w3_ref)):
            high, low = toeplitz(a, d, 128)
            ref[j, :, 0:128] = high[:, :128].astype(BF16)
            ref[j, :, 128:256] = high[:, :128].astype(BF16)
            ref[j, :, 256:384] = low[:, :128].astype(BF16)
        column_ref[j] = jnp.broadcast_to(third_ref[pl.ds(a, 1), :], (128, 128)).T
        row_ref[j] = jnp.broadcast_to(fourth_ref[pl.ds(a, 1), :], (8, 128))
        for k in range(16):
            u_ref[j, k] = first_ref[a, first_row + k // 8] + second_ref[a, second_row + k % 8]
        return carry

    lax.fori_loop(0, 4, mine, 0)


def build(order, offsets, weights, first, second, third, fourth):
    return pl.pallas_call(
        build_kernel,
        out_shape=(
            jax.ShapeDtypeStruct((2, 8, 64, 128), F32),
            jax.ShapeDtypeStruct((2, 8, 64, 128), F32),
            jax.ShapeDtypeStruct((4, 128, 384), BF16),
            jax.ShapeDtypeStruct((4, 128, 384), BF16),
            jax.ShapeDtypeStruct((4, 16), F32),
            jax.ShapeDtypeStruct((4, 128, 128), F32),
            jax.ShapeDtypeStruct((4, 8, 128), F32),
        ),
        in_specs=[SMEM] * 4 + [VMEM] * 3,
        out_specs=(VMEM, VMEM, VMEM, VMEM, SMEM, VMEM, VMEM),
        scratch_shapes=[pltpu.VMEM((8, 4, 256), F32)],
        name="build",
    )(order, offsets.T, first, second, weights, third, fourth)


def spread_kernel(vt_ref, ga_ref, gb_ref, send_sem, recv_sem, local_sem, ring_send, ring_recv):
    y, q, z, act = place()
    wide = 4 * y + q
    barrier = pltpu.get_barrier_semaphore()

    def at_a(step):
        t, p = partner(step, y, q)
        return t * 8 + p * 2 + act, {"wide": 4 * t + p, "narrow": z, "act": act}

    def at_b(step):
        t, p = partner(step, z, q)
        return 64 + t * 8 + p * 2 + act, {"wide": 4 * y + p, "narrow": t, "act": act}

    def greet(step, carry):
        pl.semaphore_signal(barrier, inc=1, device_id=at_a(step)[1], device_id_type=MESH)
        pl.semaphore_signal(barrier, inc=1, device_id=at_b(step)[1], device_id_type=MESH)
        return carry

    lax.fori_loop(1, 32, greet, 0)
    own = [
        pltpu.make_async_copy(vt_ref.at[y * 8 + q * 2 + act], ga_ref.at[z, wide], local_sem.at[0]),
        pltpu.make_async_copy(vt_ref.at[64 + z * 8 + q * 2 + act], gb_ref.at[y, 4 * z + q], local_sem.at[1]),
    ]
    for copy in own:
        copy.start()
    pl.semaphore_wait(barrier, 62)

    def send(step, carry):
        row, device = at_a(step)
        pltpu.make_async_remote_copy(
            vt_ref.at[row], ga_ref.at[z, wide], send_sem.at[0], recv_sem.at[0], device, MESH
        ).start()
        row, device = at_b(step)
        pltpu.make_async_remote_copy(
            vt_ref.at[row], gb_ref.at[y, 4 * z + q], send_sem.at[1], recv_sem.at[1], device, MESH
        ).start()
        return carry

    lax.fori_loop(1, 32, send, 0)
    for copy in own:
        copy.wait()
    streams = (
        (ga_ref, z, lambda t: {"wide": wide, "narrow": t, "act": act}),
        (gb_ref, y, lambda t: {"wide": 4 * t + q, "narrow": z, "act": act}),
    )
    for index, (ref, _, _) in enumerate(streams):
        part = ref.at[0, pl.ds(0, 31)]
        pltpu.make_async_copy(part, part, recv_sem.at[index]).wait()

    def hop(index, step, half, way):
        ref, t, device = streams[index]
        block = lax.rem(t + 8 - way * (step - 1), 8)
        piece = ref.at[block, pl.ds(16 * half, 16)]
        side = 0 if way > 0 else 1
        return pltpu.make_async_remote_copy(
            piece,
            piece,
            ring_send.at[index, step - 1, half, side],
            ring_recv.at[index, step - 1, half, side],
            device(lax.rem(t + 8 + way, 8)),
            MESH,
        )

    started = []
    for step in (1, 2, 3, 4):
        for half in (0, 1):
            for index in (0, 1):
                for way in (1, -1):
                    if step > 1 and not (step == 4 and half != (0 if way > 0 else 1)):
                        hop(index, step - 1, half, way).wait_recv()
                    if step == 4 and half != (0 if way > 0 else 1):
                        continue
                    copy = hop(index, step, half, way)
                    copy.start()
                    started.append(copy)
    for index in (0, 1):
        hop(index, 3, 1, 1).wait_recv()
        hop(index, 3, 0, -1).wait_recv()
        hop(index, 4, 0, 1).wait_recv()
        hop(index, 4, 1, -1).wait_recv()
    for copy in started:
        copy.wait_send()
    for index, (ref, _, _) in enumerate(streams):
        part = ref.at[0, pl.ds(0, 31)]
        pltpu.make_async_copy(part, part, send_sem.at[index]).wait()


def spread(vt):
    return pl.pallas_call(
        spread_kernel,
        out_shape=(jax.ShapeDtypeStruct((8, 32, 16, 128), F32),) * 2,
        in_specs=[VMEM],
        out_specs=(VMEM, VMEM),
        scratch_shapes=[
            pltpu.SemaphoreType.DMA((2,)),
            pltpu.SemaphoreType.DMA((2,)),
            pltpu.SemaphoreType.DMA((2,)),
            pltpu.SemaphoreType.DMA((2, 4, 2, 2)),
            pltpu.SemaphoreType.DMA((2, 4, 2, 2)),
        ],
        compiler_params=pltpu.CompilerParams(collective_id=0, has_side_effects=True, vmem_limit_bytes=LIMIT),
        name="spread",
    )(vt)


def stack(x):
    high, low = halves(x)
    return jnp.concatenate([high, low, high, high], axis=0)


def outer_kernel(c0_ref, c1_ref, ga_ref, gb_ref, ea_ref, eb_ref, za_ref, zb_ref):
    y, q, z, act = place()

    def wide_rows(ref, *index):
        return jnp.concatenate([ref[(half,) + index] for half in (0, 1)], axis=-1)

    def own_rows(ref, t):
        return wide_rows(ref, slice(None), pl.ds(t * 8, 8)).reshape(64, 256).astype(BF16)

    mine1 = own_rows(c1_ref, z)
    mine0 = own_rows(c0_ref, y)

    def first_a(w, carry):
        left = ga_ref[:, w, 0:8, :].reshape(64, 128)
        right = ga_ref[:, w, 8:16, :].reshape(64, 128)
        out = jnp.dot(mine1, stack(jnp.concatenate([left, right], axis=1)), preferred_element_type=F32)
        za_ref[:, pl.ds(16 * w, 8), :] = out[:, :128].reshape(8, 8, 128)
        za_ref[:, pl.ds(16 * w + 8, 8), :] = out[:, 128:].reshape(8, 8, 128)
        return carry

    lax.fori_loop(0, 32, first_a, 0, unroll=4)

    def second_a(a, carry):
        left = jnp.concatenate([wide_rows(c0_ref, a, pl.ds(half, 32, stride=2)) for half in (0, 1)], axis=0)
        left = left.astype(BF16)
        for i in range(0, 8, 2):
            right = jnp.concatenate(
                [za_ref[a, pl.ds(i, 64, stride=8), :], za_ref[a, pl.ds(i + 1, 64, stride=8), :]], axis=1
            )
            out = jnp.dot(left, stack(right), preferred_element_type=F32)
            for k in range(2):
                for half in range(2):
                    start = lax.div(a, 4) * 64 + half * 32 + (i + k) // 4 * 16 + lax.rem(a, 4) * 4 + (i + k) % 4
                    ea_ref[pl.ds(start, 32, stride=128), :] = out[
                        32 * half : 32 * half + 32, 128 * k : 128 * k + 128
                    ]
        return carry

    lax.fori_loop(0, 8, second_a, 0)

    def first_b(s, carry):
        for i in range(0, 8, 2):
            left = gb_ref[:, pl.ds(64 * s + i, 8, stride=8), :].reshape(64, 128)
            right = gb_ref[:, pl.ds(64 * s + i + 1, 8, stride=8), :].reshape(64, 128)
            out = jnp.dot(mine0, stack(jnp.concatenate([left, right], axis=1)), preferred_element_type=F32)
            zb_ref[pl.ds((8 * s + i) * 64, 64), :] = out[:, :128]
            zb_ref[pl.ds((8 * s + i + 1) * 64, 64), :] = out[:, 128:]
        return carry

    lax.fori_loop(0, 8, first_b, 0)

    def second_b(g, carry):
        for a in range(4):
            left = wide_rows(c1_ref, 4 * g + a).astype(BF16)
            for p in range(4):
                start = (4 * g + a) * 8 + 2 * p
                right = jnp.concatenate([zb_ref[pl.ds(start + k, 64, stride=64), :] for k in range(2)], axis=1)
                out = jnp.dot(left, stack(right), preferred_element_type=F32)
                for k in range(2):
                    block = out[:, 128 * k : 128 * k + 128].reshape(8, 8, 128)
                    for half in range(2):
                        eb_ref[:, p, g, 2 * k + half, 4 * a : 4 * a + 4, :] = block[:, 4 * half : 4 * half + 4]
        return carry

    lax.fori_loop(0, 2, second_b, 0)


def outer(c0, c1, ga, gb):
    ea, eb = pl.pallas_call(
        outer_kernel,
        out_shape=(
            jax.ShapeDtypeStruct((4096, 128), F32),
            jax.ShapeDtypeStruct((8, 4, 2, 4, 16, 128), F32),
        ),
        in_specs=[VMEM] * 4,
        out_specs=(VMEM, VMEM),
        scratch_shapes=[pltpu.VMEM((8, 512, 128), F32), pltpu.VMEM((4096, 128), F32)],
        compiler_params=pltpu.CompilerParams(vmem_limit_bytes=LIMIT),
        name="outer",
    )(c0, c1, ga, gb.reshape(8, 512, 128))
    return ea.reshape(32, 2, 4, 16, 128), eb


def home_kernel(
    u_ref, column_ref, row_ref, w2_ref, w3_ref, ea_ref, eb_ref,
    value_ref, prob_ref,
    r_ref, score_ref, lse_ref, other_ref, send_sem, recv_sem, local_sem, lse_send, lse_recv,
):
    y, q, z, act = place()
    wide = 4 * y + q
    row_a = y * 8 + q * 2 + act
    row_b = 64 + z * 8 + q * 2 + act
    barrier = pltpu.get_barrier_semaphore()

    def at_a(step):
        t, p = partner(lax.div(step, 2), y, q)
        g = lax.rem(act + lax.rem(step, 2), 2)
        return ea_ref.at[4 * t + p, g], {"wide": 4 * t + p, "narrow": z, "act": g}

    def at_b(step):
        t, p = partner(lax.div(step, 2), z, q)
        g = lax.rem(act + lax.rem(step, 2), 2)
        return eb_ref.at[t, p, g], {"wide": 4 * y + p, "narrow": t, "act": g}

    def greet(step, carry):
        pl.semaphore_signal(barrier, inc=1, device_id=at_a(step)[1], device_id_type=MESH)
        pl.semaphore_signal(barrier, inc=1, device_id=at_b(step)[1], device_id_type=MESH)
        return carry

    lax.fori_loop(1, 64, greet, 0)
    own = []
    for c in range(4):
        own += [
            pltpu.make_async_copy(ea_ref.at[wide, act, c], r_ref.at[c, row_a], local_sem.at[0, c]),
            pltpu.make_async_copy(eb_ref.at[z, q, act, c], r_ref.at[c, row_b], local_sem.at[1, c]),
        ]
    for copy in own:
        copy.start()
    pl.semaphore_wait(barrier, 126)

    def send_chunk(c):
        def send(step, carry):
            src, device = at_a(step)
            pltpu.make_async_remote_copy(
                src.at[c], r_ref.at[c, row_a], send_sem.at[0, c], recv_sem.at[0, c], device, MESH
            ).start()
            src, device = at_b(step)
            pltpu.make_async_remote_copy(
                src.at[c], r_ref.at[c, row_b], send_sem.at[1, c], recv_sem.at[1, c], device, MESH
            ).start()
            return carry

        lax.fori_loop(1, 64, send, 0)

    def settle(c, sem):
        for index in (0, 1):
            part = r_ref.at[c, pl.ds(0, 63)]
            pltpu.make_async_copy(part, part, sem.at[index, c]).wait()

    def swap(c):
        return pltpu.make_async_remote_copy(
            lse_ref.at[c], other_ref.at[c], lse_send.at[c], lse_recv.at[c], {"act": 1 - act}, MESH
        )

    def compute(c):
        flat = r_ref.at[c].reshape(2048, 128)
        for a in range(4):
            for j in (0, 2):
                rows = jnp.concatenate(
                    [flat[pl.ds(4 * a + j + k, 128, stride=16), :] for k in range(2)], axis=1
                )
                high, low = halves(rows)
                mid = jnp.dot(w2_ref[a], jnp.concatenate([high, low, high], axis=0), preferred_element_type=F32)
                high, low = halves(jnp.concatenate([mid[:, :128], mid[:, 128:]], axis=0))
                expected = lax.dot_general(
                    jnp.concatenate([high, low, high], axis=1),
                    w3_ref[a],
                    (((1,), (1,)), ((), ())),
                    preferred_element_type=F32,
                )
                for k in range(2):
                    util = (u_ref[a, 4 * c + j + k] + column_ref[a]) + row_ref[a, 0:1, :]
                    score_ref[a, 4 * c + j + k] = util + DISCOUNT * expected[128 * k : 128 * k + 128]

        def total(j, carry):
            scores = [score_ref[a, 4 * c + j] for a in range(4)]
            top = jnp.maximum(jnp.maximum(scores[0], scores[1]), jnp.maximum(scores[2], scores[3]))
            summed = sum(jnp.exp(s - top) for s in scores)
            lse_ref[c, j] = top + jnp.log(summed)
            return carry

        lax.fori_loop(0, 4, total, 0)

    def finish(c):
        swap(c).wait_recv()

        def one(j, carry):
            ours, theirs = lse_ref[c, j], other_ref[c, j]
            top = jnp.maximum(ours, theirs)
            value = top + jnp.log(jnp.exp(ours - top) + jnp.exp(theirs - top))
            value_ref[4 * c + j] = value
            for a in range(4):
                prob_ref[a, 4 * c + j] = jnp.exp(score_ref[a, 4 * c + j] - value).astype(BF16)
            return carry

        lax.fori_loop(0, 4, one, 0)

    send_chunk(0)
    send_chunk(1)
    for copy in own:
        copy.wait()
    for c in range(4):
        settle(c, recv_sem)
        if c < 2:
            send_chunk(c + 2)
        if c > 0:
            swap(c - 1).start()
        compute(c)
        if c > 0:
            finish(c - 1)
    swap(3).start()
    for c in range(4):
        settle(c, send_sem)
    finish(3)
    for c in range(4):
        swap(c).wait_send()


def home(u, column, row, w2, w3, ea, eb):
    return pl.pallas_call(
        home_kernel,
        out_shape=(
            jax.ShapeDtypeStruct((16, 128, 128), F32),
            jax.ShapeDtypeStruct((4, 16, 128, 128), BF16),
        ),
        in_specs=[SMEM] + [VMEM] * 6,
        out_specs=(VMEM, VMEM),
        scratch_shapes=[
            pltpu.VMEM((4, 128, 16, 128), F32),
            pltpu.VMEM((4, 16, 128, 128), F32),
            pltpu.VMEM((4, 4, 128, 128), F32),
            pltpu.VMEM((4, 4, 128, 128), F32),
            pltpu.SemaphoreType.DMA((2, 4)),
            pltpu.SemaphoreType.DMA((2, 4)),
            pltpu.SemaphoreType.DMA((2, 4)),
            pltpu.SemaphoreType.DMA((4,)),
            pltpu.SemaphoreType.DMA((4,)),
        ],
        compiler_params=pltpu.CompilerParams(collective_id=1, has_side_effects=True, vmem_limit_bytes=LIMIT),
        name="home",
    )(u, column, row, w2, w3, ea, eb)


def body(
    value_now,
    cost_first,
    cost_second,
    cost_third,
    cost_fourth,
    trans_weights,
    trans_offsets,
    action_order,
):
    c0, c1, w2, w3, u, column, row = build(
        action_order, trans_offsets, trans_weights, cost_first, cost_second, cost_third, cost_fourth
    )
    vt = value_now.transpose(2, 0, 1, 3).reshape(128, 16, 128)
    ga, gb = spread(vt)
    ea, eb = outer(c0, c1, ga, gb)
    new_value, choice_prob = home(u, column, row, w2, w3, ea, eb)
    return new_value.reshape(2, 8, 128, 128), choice_prob.reshape(4, 2, 8, 128, 128)


def solution(mesh):
    return jax.shard_map(
        body,
        mesh=mesh,
        in_specs=(P("wide", "narrow", None, None), P(), P(), P(), P(), P(), P(), P()),
        out_specs=(P("wide", "narrow", None, None), P("act", "wide", "narrow", None, None)),
        check_vma=False,
    )
```

```python
import jax
import jax.numpy as jnp
from jax import lax
from jax.experimental import pallas as pl
from jax.experimental.pallas import tpu as pltpu
from jax.sharding import PartitionSpec as P

DISCOUNT = 0.95
MESH = pl.DeviceIdType.MESH
F32 = jnp.float32
BF16 = jnp.bfloat16
VMEM = pl.BlockSpec(memory_space=pltpu.VMEM)
SMEM = pl.BlockSpec(memory_space=pltpu.SMEM)
LIMIT = 34 * 1024 * 1024


def place():
    wide = lax.axis_index("wide")
    return lax.div(wide, 4), lax.rem(wide, 4), lax.axis_index("narrow"), lax.axis_index("act")


def partner(step, t, q, sign):
    near = lax.rem(step, 8)
    far = lax.div(near + 1, 2)
    shift = sign * (1 - 2 * lax.rem(near + 1, 2)) * far
    mixed = lax.div(step, 8) + near
    return lax.rem(t + shift + 8, 8), mixed


def halves(x):
    high = x.astype(BF16)
    low = (x - high.astype(F32)).astype(BF16)
    return high, low


def builders(
    order_ref, offs_ref, first_ref, second_ref, w_ref, third_ref, fourth_ref,
    c0_ref, c1_ref, w2_ref, w3_ref, u_ref, column_ref, row_ref, pad_ref,
):
    act = lax.axis_index("act")
    first_row = lax.axis_index("wide") * 2
    second_row = lax.axis_index("narrow") * 8
    number = lax.broadcasted_iota(jnp.int32, (16, 256), 0)
    lane = lax.broadcasted_iota(jnp.int32, (16, 256), 1)
    zero = jnp.zeros((16, 256), F32)

    def prepare():
        pad_ref[...] = jnp.zeros_like(pad_ref)
        taps = w_ref[...]
        pad_ref[:, :, 0:65] = taps / jnp.sum(taps, axis=2, keepdims=True)

    def toeplitz(a, d, length, store):
        row = pad_ref[pl.ds(a, 1), d, :]
        shift = lax.rem(offs_ref[d, a] - 32 + 256, 256)
        base = pltpu.roll(jnp.broadcast_to(row, (16, 256)), shift, 1)
        for bit in (1, 2, 4, 8):
            base = jnp.where((number & bit) != 0, pltpu.roll(base, bit, 1), base)
        for start in range(0, length, 16):
            spread = pltpu.roll(base, start, 1) if start else base
            below = jnp.sum(jnp.where(lane >= 192, spread, zero), axis=1, keepdims=True)
            above = jnp.sum(jnp.where((lane >= length) & (lane < 192), spread, zero), axis=1, keepdims=True)
            full = jnp.where(lane == 0, spread + below, jnp.where(lane == length - 1, spread + above, spread))
            full = jnp.where(lane < length, full, zero)
            high = full.astype(BF16).astype(F32)
            store(pl.ds(start, 16), high, full - high)

    def outer(j, carry):
        a = order_ref[j]
        for d, ref in ((0, c0_ref), (1, c1_ref)):

            def store(rows, high, low):
                both = high + pltpu.roll(high, 64, 1) + pltpu.roll(low, 128, 1)
                ref[0, j, rows] = both[:, :128]
                ref[1, j, rows] = both[:, 128:]

            toeplitz(a, d, 64, store)
        return carry

    def inner(j, carry):
        a = order_ref[act * 4 + j]
        for d, ref in ((2, w2_ref), (3, w3_ref)):

            def store(rows, high, low):
                ref[j, rows, 0:128] = high[:, :128].astype(BF16)
                ref[j, rows, 128:256] = high[:, :128].astype(BF16)
                ref[j, rows, 256:384] = low[:, :128].astype(BF16)

            toeplitz(a, d, 128, store)
        column_ref[j] = jnp.broadcast_to(third_ref[pl.ds(a, 1), :], (128, 128)).T
        row_ref[j] = jnp.broadcast_to(fourth_ref[pl.ds(a, 1), :], (8, 128))
        for k in range(16):
            u_ref[j, k] = first_ref[a, first_row + k // 8] + second_ref[a, second_row + k % 8]
        return carry

    return prepare, outer, inner


def stack(x):
    high, low = halves(x)
    return jnp.concatenate([high, low, high, high], axis=0)


def wide_rows(ref, *index):
    return jnp.concatenate([ref[(half,) + index] for half in (0, 1)], axis=-1)


def step_kernel(
    order_ref, offs_ref, cost0_ref, cost1_ref, taps_ref, cost2_ref, cost3_ref, v_ref,
    value_ref, prob_ref,
    c0_ref, c1_ref, w2_ref, w3_ref, u_ref, column_ref, row_ref, pad_ref,
    vt_ref, ga_ref, gb_ref, za_ref, zb_ref, ea_ref, eb_ref, r_ref, score_ref, lse_ref, other_ref,
    first_send, first_recv, first_local, ring_send, ring_recv,
    send_sem, recv_sem, local_sem, lse_send, lse_recv,
):
    y, q, z, act = place()
    wide = 4 * y + q
    row_a = y * 8 + q * 2 + act
    row_b = 64 + z * 8 + q * 2 + act
    barrier = pltpu.get_barrier_semaphore()
    prepare, build_outer, build_inner = builders(
        order_ref, offs_ref, cost0_ref, cost1_ref, taps_ref, cost2_ref, cost3_ref,
        c0_ref, c1_ref, w2_ref, w3_ref, u_ref, column_ref, row_ref, pad_ref,
    )

    def home_a(step):
        t, mixed = partner(step, y, q, 1)
        p = lax.rem(q + lax.rem(lax.div(mixed, 2), 4), 4)
        g = lax.rem(act + lax.rem(mixed, 2), 2)
        return ea_ref.at[4 * t + p, g], {"wide": 4 * t + p, "narrow": z, "act": g}

    def home_b(step):
        t, mixed = partner(step, z, q, -1)
        p = lax.rem(q + lax.rem(lax.div(mixed, 2), 4), 4)
        g = lax.rem(act + lax.rem(mixed, 2), 2)
        return eb_ref.at[t, p, g], {"wide": 4 * y + p, "narrow": t, "act": g}

    def greet(step, carry):
        pl.semaphore_signal(barrier, inc=1, device_id=home_a(step)[1], device_id_type=MESH)
        pl.semaphore_signal(barrier, inc=1, device_id=home_b(step)[1], device_id_type=MESH)
        return carry

    lax.fori_loop(1, 64, greet, 0)

    def pick(n, carry):
        for half in (0, 1):
            vt_ref[half, n] = v_ref[pl.ds(64 * half + 2 * n + act, 16, stride=128), :]
        return carry

    lax.fori_loop(0, 32, pick, 0, unroll=4)
    prepare()
    pl.semaphore_wait(barrier, 126)

    def first(step, carry):
        t, mixed = partner(step, y, q, 1)
        p = lax.rem(q + lax.rem(mixed, 4), 4)
        pltpu.make_async_remote_copy(
            vt_ref.at[0, 4 * t + p],
            ga_ref.at[z, wide],
            first_send.at[0],
            first_recv.at[0],
            {"wide": 4 * t + p, "narrow": z, "act": act},
            MESH,
        ).start()
        t, mixed = partner(step, z, q, -1)
        p = lax.rem(q + lax.rem(mixed, 4), 4)
        pltpu.make_async_remote_copy(
            vt_ref.at[1, 4 * t + p],
            gb_ref.at[y, 4 * z + q],
            first_send.at[1],
            first_recv.at[1],
            {"wide": 4 * y + p, "narrow": t, "act": act},
            MESH,
        ).start()
        return carry

    lax.fori_loop(1, 32, first, 0)
    own = [
        pltpu.make_async_copy(vt_ref.at[0, wide], ga_ref.at[z, wide], first_local.at[0]),
        pltpu.make_async_copy(vt_ref.at[1, 4 * z + q], gb_ref.at[y, 4 * z + q], first_local.at[1]),
    ]
    for copy in own:
        copy.start()
    lax.fori_loop(0, 4, build_outer, 0, unroll=2)
    for copy in own:
        copy.wait()
    streams = (
        (ga_ref, z, lambda t: {"wide": wide, "narrow": t, "act": act}),
        (gb_ref, y, lambda t: {"wide": 4 * t + q, "narrow": z, "act": act}),
    )
    for index, (ref, _, _) in enumerate(streams):
        part = ref.at[0, pl.ds(0, 31)]
        pltpu.make_async_copy(part, part, first_recv.at[index]).wait()

    def hop(index, step, half, way):
        ref, t, device = streams[index]
        block = lax.rem(t + 8 - way * (step - 1), 8)
        piece = ref.at[block, pl.ds(16 * half, 16)]
        side = 0 if way > 0 else 1
        return pltpu.make_async_remote_copy(
            piece,
            piece,
            ring_send.at[index, step - 1, half, side],
            ring_recv.at[index, step - 1, half, side],
            device(lax.rem(t + 8 + way, 8)),
            MESH,
        )

    started = []
    for step in (1, 2, 3, 4):
        for half in (0, 1):
            for index in (0, 1):
                for way in (1, -1):
                    if step == 4 and half != (0 if way > 0 else 1):
                        continue
                    if step > 1:
                        hop(index, step - 1, half, way).wait_recv()
                    copy = hop(index, step, half, way)
                    copy.start()
                    started.append(copy)
        if step == 1:
            lax.fori_loop(4, 8, build_outer, 0, unroll=2)
        if step == 2:
            lax.fori_loop(0, 2, build_inner, 0, unroll=2)
        if step == 3:
            lax.fori_loop(2, 4, build_inner, 0, unroll=2)
    for index in (0, 1):
        hop(index, 3, 1, 1).wait_recv()
        hop(index, 3, 0, -1).wait_recv()
        hop(index, 4, 0, 1).wait_recv()
        hop(index, 4, 1, -1).wait_recv()

    def own_rows(ref, t):
        return wide_rows(ref, slice(None), pl.ds(t * 8, 8)).reshape(64, 256).astype(BF16)

    mine1 = own_rows(c1_ref, z)
    mine0 = own_rows(c0_ref, y)
    gb_rows = gb_ref.reshape(8, 512, 128)

    def first_a(w, carry):
        left = ga_ref[:, w, 0:8, :].reshape(64, 128)
        right = ga_ref[:, w, 8:16, :].reshape(64, 128)
        out = jnp.dot(mine1, stack(jnp.concatenate([left, right], axis=1)), preferred_element_type=F32)
        za_ref[:, pl.ds(16 * w, 8), :] = out[:, :128].reshape(8, 8, 128)
        za_ref[:, pl.ds(16 * w + 8, 8), :] = out[:, 128:].reshape(8, 8, 128)
        return carry


    def first_b(s, carry):
        for i in range(0, 8, 2):
            left = gb_rows[:, pl.ds(64 * s + i, 8, stride=8), :].reshape(64, 128)
            right = gb_rows[:, pl.ds(64 * s + i + 1, 8, stride=8), :].reshape(64, 128)
            out = jnp.dot(mine0, stack(jnp.concatenate([left, right], axis=1)), preferred_element_type=F32)
            zb_ref[pl.ds((8 * s + i) * 64, 64), :] = out[:, :128]
            zb_ref[pl.ds((8 * s + i + 1) * 64, 64), :] = out[:, 128:]
        return carry

    ea_rows = ea_ref.reshape(4096, 128)

    def second_a(part):
        def one(a, carry):
            left = jnp.concatenate([wide_rows(c0_ref, a, pl.ds(half, 32, stride=2)) for half in (0, 1)], axis=0)
            left = left.astype(BF16)
            for i in (0, 2):
                right = jnp.concatenate(
                    [za_ref[a, pl.ds(4 * part + i + k, 64, stride=8), :] for k in range(2)], axis=1
                )
                out = jnp.dot(left, stack(right), preferred_element_type=F32)
                for k in range(2):
                    for half in range(2):
                        start = lax.div(a, 4) * 64 + half * 32 + part * 16 + lax.rem(a, 4) * 4 + i + k
                        ea_rows[pl.ds(start, 32, stride=128), :] = out[
                            32 * half : 32 * half + 32, 128 * k : 128 * k + 128
                        ]
            return carry

        lax.fori_loop(0, 8, one, 0, unroll=2)

    def second_b(half):
        def one(g, carry):
            for a in range(4):
                left = wide_rows(c1_ref, 4 * g + a).astype(BF16)
                for p in (0, 2):
                    start = (4 * g + a) * 8 + 2 * p + half
                    right = jnp.concatenate(
                        [zb_ref[pl.ds(start + 2 * k, 64, stride=64), :] for k in range(2)], axis=1
                    )
                    out = jnp.dot(left, stack(right), preferred_element_type=F32)
                    for k in range(2):
                        block = out[:, 128 * k : 128 * k + 128].reshape(8, 8, 128)
                        for part in range(2):
                            eb_ref[:, p + k, g, 2 * half + part, 4 * a : 4 * a + 4, :] = block[
                                :, 4 * part : 4 * part + 4
                            ]
            return carry

        lax.fori_loop(0, 2, one, 0)

    def send_a(c):
        pltpu.make_async_copy(ea_ref.at[wide, act, c], r_ref.at[c, row_a], local_sem.at[0, c]).start()

        def send(step, carry):
            src, device = home_a(step)
            pltpu.make_async_remote_copy(
                src.at[c], r_ref.at[c, row_a], send_sem.at[0, c], recv_sem.at[0, c], device, MESH
            ).start()
            return carry

        lax.fori_loop(1, 64, send, 0)

    def send_b(c):
        pltpu.make_async_copy(eb_ref.at[z, q, act, c], r_ref.at[c, row_b], local_sem.at[1, c]).start()

        def send(step, carry):
            src, device = home_b(step)
            pltpu.make_async_remote_copy(
                src.at[c], r_ref.at[c, row_b], send_sem.at[1, c], recv_sem.at[1, c], device, MESH
            ).start()
            return carry

        lax.fori_loop(1, 64, send, 0)

    def settle(c, sem):
        for index in (0, 1):
            part = r_ref.at[c, pl.ds(0, 63)]
            pltpu.make_async_copy(part, part, sem.at[index, c]).wait()

    def arrive(c):
        pltpu.make_async_copy(ea_ref.at[wide, act, c], r_ref.at[c, row_a], local_sem.at[0, c]).wait()
        pltpu.make_async_copy(eb_ref.at[z, q, act, c], r_ref.at[c, row_b], local_sem.at[1, c]).wait()
        settle(c, recv_sem)

    def swap(n):
        return pltpu.make_async_remote_copy(
            lse_ref.at[n], other_ref.at[n], lse_send.at[n], lse_recv.at[n], {"act": 1 - act}, MESH
        )

    def compute(n):
        flat = r_ref.at[n // 2].reshape(2048, 128)
        for a in range(4):
            rows = jnp.concatenate(
                [flat[pl.ds(4 * a + 2 * (n % 2) + k, 128, stride=16), :] for k in range(2)], axis=1
            )
            high, low = halves(rows)
            mid = jnp.dot(w2_ref[a], jnp.concatenate([high, low, high], axis=0), preferred_element_type=F32)
            high, low = halves(jnp.concatenate([mid[:, :128], mid[:, 128:]], axis=0))
            expected = lax.dot_general(
                jnp.concatenate([high, low, high], axis=1),
                w3_ref[a],
                (((1,), (1,)), ((), ())),
                preferred_element_type=F32,
            )
            for k in range(2):
                util = (u_ref[a, 2 * n + k] + column_ref[a]) + row_ref[a, 0:1, :]
                score_ref[a, 2 * n + k] = util + DISCOUNT * expected[128 * k : 128 * k + 128]
        for k in range(2):
            scores = [score_ref[a, 2 * n + k] for a in range(4)]
            top = jnp.maximum(jnp.maximum(scores[0], scores[1]), jnp.maximum(scores[2], scores[3]))
            summed = sum(jnp.exp(s - top) for s in scores)
            lse_ref[n, k] = top + jnp.log(summed)

    def finish(n):
        swap(n).wait_recv()
        for k in range(2):
            ours, theirs = lse_ref[n, k], other_ref[n, k]
            top = jnp.maximum(ours, theirs)
            value = top + jnp.log(jnp.exp(ours - top) + jnp.exp(theirs - top))
            value_ref[2 * n + k] = value
            for a in range(4):
                prob_ref[a, 2 * n + k] = jnp.exp(score_ref[a, 2 * n + k] - value).astype(BF16)

    lax.fori_loop(0, 32, first_a, 0, unroll=4)
    second_a(0)
    send_a(0)
    lax.fori_loop(0, 8, first_b, 0)
    second_b(0)
    send_b(0)
    second_a(1)
    send_a(1)
    send_b(1)
    second_b(1)
    for c in (2, 3):
        send_a(c)
        send_b(c)
    for c in range(4):
        arrive(c)
        for n in (2 * c, 2 * c + 1):
            compute(n)
            if n > 0:
                swap(n - 1).start()
            if n > 2:
                finish(n - 3)
    swap(7).start()
    for c in range(4):
        settle(c, send_sem)
    for index, (ref, _, _) in enumerate(streams):
        part = ref.at[0, pl.ds(0, 31)]
        pltpu.make_async_copy(part, part, first_send.at[index]).wait()
    for copy in started:
        copy.wait_send()
    for n in (5, 6, 7):
        finish(n)
    for n in range(8):
        swap(n).wait_send()


def whole(order, offsets, weights, first, second, third, fourth, v):
    dma = pltpu.SemaphoreType.DMA
    return pl.pallas_call(
        step_kernel,
        out_shape=(
            jax.ShapeDtypeStruct((16, 128, 128), F32),
            jax.ShapeDtypeStruct((4, 16, 128, 128), BF16),
        ),
        in_specs=[SMEM] * 4 + [VMEM] * 4,
        out_specs=(VMEM, VMEM),
        scratch_shapes=[
            pltpu.VMEM((2, 8, 64, 128), F32),
            pltpu.VMEM((2, 8, 64, 128), F32),
            pltpu.VMEM((4, 128, 384), BF16),
            pltpu.VMEM((4, 128, 384), BF16),
            pltpu.SMEM((4, 16), F32),
            pltpu.VMEM((4, 128, 128), F32),
            pltpu.VMEM((4, 8, 128), F32),
            pltpu.VMEM((8, 4, 256), F32),
            pltpu.VMEM((2, 32, 16, 128), F32),
            pltpu.VMEM((8, 32, 16, 128), F32),
            pltpu.VMEM((8, 32, 16, 128), F32),
            pltpu.VMEM((8, 512, 128), F32),
            pltpu.VMEM((4096, 128), F32),
            pltpu.VMEM((32, 2, 4, 16, 128), F32),
            pltpu.VMEM((8, 4, 2, 4, 16, 128), F32),
            pltpu.VMEM((4, 128, 16, 128), F32),
            pltpu.VMEM((4, 16, 128, 128), F32),
            pltpu.VMEM((8, 2, 128, 128), F32),
            pltpu.VMEM((8, 2, 128, 128), F32),
            dma((2,)),
            dma((2,)),
            dma((2,)),
            dma((2, 4, 2, 2)),
            dma((2, 4, 2, 2)),
            dma((2, 4)),
            dma((2, 4)),
            dma((2, 4)),
            dma((8,)),
            dma((8,)),
        ],
        compiler_params=pltpu.CompilerParams(collective_id=0, has_side_effects=True, vmem_limit_bytes=LIMIT),
        name="step",
    )(order, offsets.T, first, second, weights, third, fourth, v)


def body(
    value_now,
    cost_first,
    cost_second,
    cost_third,
    cost_fourth,
    trans_weights,
    trans_offsets,
    action_order,
):
    new_value, choice_prob = whole(
        action_order,
        trans_offsets,
        trans_weights,
        cost_first,
        cost_second,
        cost_third,
        cost_fourth,
        value_now.reshape(2048, 128),
    )
    return new_value.reshape(2, 8, 128, 128), choice_prob.reshape(4, 2, 8, 128, 128)


def solution(mesh):
    return jax.shard_map(
        body,
        mesh=mesh,
        in_specs=(P("wide", "narrow", None, None), P(), P(), P(), P(), P(), P(), P()),
        out_specs=(P("wide", "narrow", None, None), P("act", "wide", "narrow", None, None)),
        check_vma=False,
    )
```

```python
import jax
import jax.numpy as jnp
from jax import lax
from jax.experimental import pallas as pl
from jax.experimental.pallas import tpu as pltpu
from jax.sharding import PartitionSpec as P

DISCOUNT = 0.95
MESH = pl.DeviceIdType.MESH
F32 = jnp.float32
BF16 = jnp.bfloat16
VMEM = pl.BlockSpec(memory_space=pltpu.VMEM)
SMEM = pl.BlockSpec(memory_space=pltpu.SMEM)
LIMIT = 56 * 1024 * 1024


def place():
    wide = lax.axis_index("wide")
    return lax.div(wide, 4), lax.rem(wide, 4), lax.axis_index("narrow"), lax.axis_index("act")


def partner(step, t, q, sign):
    near = lax.rem(step, 8)
    far = lax.div(near + 1, 2)
    shift = sign * (1 - 2 * lax.rem(near + 1, 2)) * far
    mixed = lax.div(step, 8) + near
    return lax.rem(t + shift + 8, 8), mixed


def halves(x):
    high = x.astype(BF16)
    low = (x - high.astype(F32)).astype(BF16)
    return high, low


def builders(
    order_ref, offs_ref, first_ref, second_ref, w_ref, third_ref, fourth_ref,
    c0_ref, c1_ref, w2_ref, w3_ref, u_ref, column_ref, row_ref, pad_ref,
):
    act = lax.axis_index("act")
    first_row = lax.axis_index("wide") * 2
    second_row = lax.axis_index("narrow") * 8
    number = lax.broadcasted_iota(jnp.int32, (16, 256), 0)
    lane = lax.broadcasted_iota(jnp.int32, (16, 256), 1)
    zero = jnp.zeros((16, 256), F32)

    def prepare():
        pad_ref[...] = jnp.zeros_like(pad_ref)
        taps = w_ref[...]
        pad_ref[:, :, 0:65] = taps / jnp.sum(taps, axis=2, keepdims=True)

    def toeplitz(a, d, length, store):
        row = pad_ref[pl.ds(a, 1), d, :]
        shift = lax.rem(offs_ref[d, a] - 32 + 256, 256)
        base = pltpu.roll(jnp.broadcast_to(row, (16, 256)), shift, 1)
        for bit in (1, 2, 4, 8):
            base = jnp.where((number & bit) != 0, pltpu.roll(base, bit, 1), base)
        for start in range(0, length, 16):
            spread = pltpu.roll(base, start, 1) if start else base
            below = jnp.sum(jnp.where(lane >= 192, spread, zero), axis=1, keepdims=True)
            above = jnp.sum(jnp.where((lane >= length) & (lane < 192), spread, zero), axis=1, keepdims=True)
            full = jnp.where(lane == 0, spread + below, jnp.where(lane == length - 1, spread + above, spread))
            full = jnp.where(lane < length, full, zero)
            high = full.astype(BF16).astype(F32)
            store(pl.ds(start, 16), high, full - high)

    def outer(j, carry):
        a = order_ref[j]
        for d, ref in ((0, c0_ref), (1, c1_ref)):

            def store(rows, high, low):
                both = high + pltpu.roll(high, 64, 1) + pltpu.roll(low, 128, 1)
                ref[0, j, rows] = both[:, :128]
                ref[1, j, rows] = both[:, 128:]

            toeplitz(a, d, 64, store)
        return carry

    def inner(j, carry):
        a = order_ref[act * 4 + j]
        for d, ref in ((2, w2_ref), (3, w3_ref)):

            def store(rows, high, low):
                ref[j, rows, 0:128] = high[:, :128].astype(BF16)
                ref[j, rows, 128:256] = high[:, :128].astype(BF16)
                ref[j, rows, 256:384] = low[:, :128].astype(BF16)

            toeplitz(a, d, 128, store)
        column_ref[j] = jnp.broadcast_to(third_ref[pl.ds(a, 1), :], (128, 128)).T
        row_ref[j] = jnp.broadcast_to(fourth_ref[pl.ds(a, 1), :], (8, 128))
        for k in range(16):
            u_ref[j, k] = first_ref[a, first_row + k // 8] + second_ref[a, second_row + k % 8]
        return carry

    return prepare, outer, inner


def stack(x):
    high, low = halves(x)
    return jnp.concatenate([high, low, high, high], axis=0)


def wide_rows(ref, *index):
    return jnp.concatenate([ref[(half,) + index] for half in (0, 1)], axis=-1)


def step_kernel(
    order_in, offs_in, cost0_in, cost1_in, taps_in, cost2_in, cost3_in, v_in,
    value_out, prob_out,
    value_ref, prob_ref, store_sem,
    order_ref, offs_ref, cost0_ref, cost1_ref, taps_ref, cost2_ref, cost3_ref, v_ref, load_sem,
    c0_ref, c1_ref, w2_ref, w3_ref, u_ref, column_ref, row_ref, pad_ref,
    vt_ref, ga_ref, gb_ref, za_ref, zb_ref, ea_ref, eb_ref, r_ref, score_ref, lse_ref, other_ref,
    first_send, first_recv, first_local, ring_send, ring_recv,
    send_sem, recv_sem, local_sem, lse_send, lse_recv,
):
    y, q, z, act = place()
    wide = 4 * y + q
    row_a = y * 8 + q * 2 + act
    row_b = 64 + z * 8 + q * 2 + act
    barrier = pltpu.get_barrier_semaphore()
    loads = [
        pltpu.make_async_copy(src, dst, load_sem.at[n])
        for n, (src, dst) in enumerate(
            (
                (v_in, v_ref),
                (taps_in, taps_ref),
                (order_in, order_ref),
                (offs_in, offs_ref),
                (cost0_in, cost0_ref),
                (cost1_in, cost1_ref),
                (cost2_in, cost2_ref),
                (cost3_in, cost3_ref),
            )
        )
    ]
    for load in loads:
        load.start()
    prepare, build_outer, build_inner = builders(
        order_ref, offs_ref, cost0_ref, cost1_ref, taps_ref, cost2_ref, cost3_ref,
        c0_ref, c1_ref, w2_ref, w3_ref, u_ref, column_ref, row_ref, pad_ref,
    )

    def home_a(step):
        t, mixed = partner(step, y, q, 1)
        p = lax.rem(q + lax.rem(lax.div(mixed, 2), 4), 4)
        g = lax.rem(act + lax.rem(mixed, 2), 2)
        return ea_ref.at[4 * t + p, g], {"wide": 4 * t + p, "narrow": z, "act": g}

    def home_b(step):
        t, mixed = partner(step, z, q, -1)
        p = lax.rem(q + lax.rem(lax.div(mixed, 2), 4), 4)
        g = lax.rem(act + lax.rem(mixed, 2), 2)
        return eb_ref.at[t, p, g], {"wide": 4 * y + p, "narrow": t, "act": g}

    def greet(step, carry):
        pl.semaphore_signal(barrier, inc=1, device_id=home_a(step)[1], device_id_type=MESH)
        pl.semaphore_signal(barrier, inc=1, device_id=home_b(step)[1], device_id_type=MESH)
        return carry

    lax.fori_loop(1, 64, greet, 0, unroll=3)
    for load in loads:
        load.wait()

    def pick(n, carry):
        for half in (0, 1):
            vt_ref[half, n] = v_ref[pl.ds(64 * half + 2 * n + act, 16, stride=128), :]
        return carry

    lax.fori_loop(0, 32, pick, 0, unroll=4)
    prepare()
    pl.semaphore_wait(barrier, 126)

    def first(step, carry):
        t, mixed = partner(step, y, q, 1)
        p = lax.rem(q + lax.rem(mixed, 4), 4)
        pltpu.make_async_remote_copy(
            vt_ref.at[0, 4 * t + p],
            ga_ref.at[z, wide],
            first_send.at[0],
            first_recv.at[0],
            {"wide": 4 * t + p, "narrow": z, "act": act},
            MESH,
        ).start()
        t, mixed = partner(step, z, q, -1)
        p = lax.rem(q + lax.rem(mixed, 4), 4)
        pltpu.make_async_remote_copy(
            vt_ref.at[1, 4 * t + p],
            gb_ref.at[y, 4 * z + q],
            first_send.at[1],
            first_recv.at[1],
            {"wide": 4 * y + p, "narrow": t, "act": act},
            MESH,
        ).start()
        return carry

    lax.fori_loop(1, 32, first, 0)
    own = [
        pltpu.make_async_copy(vt_ref.at[0, wide], ga_ref.at[z, wide], first_local.at[0]),
        pltpu.make_async_copy(vt_ref.at[1, 4 * z + q], gb_ref.at[y, 4 * z + q], first_local.at[1]),
    ]
    for copy in own:
        copy.start()
    lax.fori_loop(0, 4, build_outer, 0, unroll=2)
    for copy in own:
        copy.wait()
    streams = (
        (ga_ref, z, lambda t: {"wide": wide, "narrow": t, "act": act}),
        (gb_ref, y, lambda t: {"wide": 4 * t + q, "narrow": z, "act": act}),
    )
    for index, (ref, _, _) in enumerate(streams):
        part = ref.at[0, pl.ds(0, 31)]
        pltpu.make_async_copy(part, part, first_recv.at[index]).wait()

    def hop(index, step, half, way):
        ref, t, device = streams[index]
        block = lax.rem(t + 8 - way * (step - 1), 8)
        piece = ref.at[block, pl.ds(16 * half, 16)]
        side = 0 if way > 0 else 1
        return pltpu.make_async_remote_copy(
            piece,
            piece,
            ring_send.at[index, step - 1, half, side],
            ring_recv.at[index, step - 1, half, side],
            device(lax.rem(t + 8 + way, 8)),
            MESH,
        )

    started = []
    for step in (1, 2, 3, 4):
        for half in (0, 1):
            for index in (0, 1):
                for way in (1, -1):
                    if step == 4 and half != (0 if way > 0 else 1):
                        continue
                    if step > 1:
                        hop(index, step - 1, half, way).wait_recv()
                    copy = hop(index, step, half, way)
                    copy.start()
                    started.append(copy)
        if step == 1:
            lax.fori_loop(4, 8, build_outer, 0, unroll=2)
        if step == 2:
            lax.fori_loop(0, 2, build_inner, 0, unroll=2)
        if step == 3:
            lax.fori_loop(2, 4, build_inner, 0, unroll=2)
    for index in (0, 1):
        hop(index, 3, 1, 1).wait_recv()
        hop(index, 3, 0, -1).wait_recv()
        hop(index, 4, 0, 1).wait_recv()
        hop(index, 4, 1, -1).wait_recv()

    def own_rows(ref, t):
        return wide_rows(ref, slice(None), pl.ds(t * 8, 8)).reshape(64, 256).astype(BF16)

    mine1 = own_rows(c1_ref, z)
    mine0 = own_rows(c0_ref, y)
    gb_rows = gb_ref.reshape(8, 512, 128)

    def first_a(w, carry):
        left = ga_ref[:, w, 0:8, :].reshape(64, 128)
        right = ga_ref[:, w, 8:16, :].reshape(64, 128)
        out = jnp.dot(mine1, stack(jnp.concatenate([left, right], axis=1)), preferred_element_type=F32)
        za_ref[:, pl.ds(16 * w, 8), :] = out[:, :128].reshape(8, 8, 128)
        za_ref[:, pl.ds(16 * w + 8, 8), :] = out[:, 128:].reshape(8, 8, 128)
        return carry


    def first_b(s, carry):
        for i in range(0, 8, 2):
            left = gb_rows[:, pl.ds(64 * s + i, 8, stride=8), :].reshape(64, 128)
            right = gb_rows[:, pl.ds(64 * s + i + 1, 8, stride=8), :].reshape(64, 128)
            out = jnp.dot(mine0, stack(jnp.concatenate([left, right], axis=1)), preferred_element_type=F32)
            zb_ref[pl.ds((8 * s + i) * 64, 64), :] = out[:, :128]
            zb_ref[pl.ds((8 * s + i + 1) * 64, 64), :] = out[:, 128:]
        return carry

    ea_rows = ea_ref.reshape(4096, 128)

    def second_a(part):
        def one(a, carry):
            left = jnp.concatenate([wide_rows(c0_ref, a, pl.ds(half, 32, stride=2)) for half in (0, 1)], axis=0)
            left = left.astype(BF16)
            for i in (0, 2):
                right = jnp.concatenate(
                    [za_ref[a, pl.ds(4 * part + i + k, 64, stride=8), :] for k in range(2)], axis=1
                )
                out = jnp.dot(left, stack(right), preferred_element_type=F32)
                for k in range(2):
                    for half in range(2):
                        start = lax.div(a, 4) * 64 + half * 32 + part * 16 + lax.rem(a, 4) * 4 + i + k
                        ea_rows[pl.ds(start, 32, stride=128), :] = out[
                            32 * half : 32 * half + 32, 128 * k : 128 * k + 128
                        ]
            return carry

        lax.fori_loop(0, 8, one, 0, unroll=2)

    def second_b(half):
        def one(g, carry):
            for a in range(4):
                left = wide_rows(c1_ref, 4 * g + a).astype(BF16)
                for p in (0, 2):
                    start = (4 * g + a) * 8 + 2 * p + half
                    right = jnp.concatenate(
                        [zb_ref[pl.ds(start + 2 * k, 64, stride=64), :] for k in range(2)], axis=1
                    )
                    out = jnp.dot(left, stack(right), preferred_element_type=F32)
                    for k in range(2):
                        block = out[:, 128 * k : 128 * k + 128].reshape(8, 8, 128)
                        for part in range(2):
                            eb_ref[:, p + k, g, 2 * half + part, 4 * a : 4 * a + 4, :] = block[
                                :, 4 * part : 4 * part + 4
                            ]
            return carry

        lax.fori_loop(0, 2, one, 0)

    def send_a(c):
        pltpu.make_async_copy(ea_ref.at[wide, act, c], r_ref.at[c, row_a], local_sem.at[0, c]).start()

        def send(step, carry):
            src, device = home_a(step)
            pltpu.make_async_remote_copy(
                src.at[c], r_ref.at[c, row_a], send_sem.at[0, c], recv_sem.at[0, c], device, MESH
            ).start()
            return carry

        lax.fori_loop(1, 64, send, 0, unroll=3)

    def send_b(c):
        pltpu.make_async_copy(eb_ref.at[z, q, act, c], r_ref.at[c, row_b], local_sem.at[1, c]).start()

        def send(step, carry):
            src, device = home_b(step)
            pltpu.make_async_remote_copy(
                src.at[c], r_ref.at[c, row_b], send_sem.at[1, c], recv_sem.at[1, c], device, MESH
            ).start()
            return carry

        lax.fori_loop(1, 64, send, 0, unroll=3)

    def settle(c, sem):
        for index in (0, 1):
            part = r_ref.at[c, pl.ds(0, 63)]
            pltpu.make_async_copy(part, part, sem.at[index, c]).wait()

    def arrive(c):
        pltpu.make_async_copy(ea_ref.at[wide, act, c], r_ref.at[c, row_a], local_sem.at[0, c]).wait()
        pltpu.make_async_copy(eb_ref.at[z, q, act, c], r_ref.at[c, row_b], local_sem.at[1, c]).wait()
        settle(c, recv_sem)

    def swap(n):
        return pltpu.make_async_remote_copy(
            lse_ref.at[n], other_ref.at[n], lse_send.at[n], lse_recv.at[n], {"act": 1 - act}, MESH
        )

    def compute(n):
        flat = r_ref.at[n // 2].reshape(2048, 128)
        for a in range(4):
            rows = jnp.concatenate(
                [flat[pl.ds(4 * a + 2 * (n % 2) + k, 128, stride=16), :] for k in range(2)], axis=1
            )
            high, low = halves(rows)
            mid = jnp.dot(w2_ref[a], jnp.concatenate([high, low, high], axis=0), preferred_element_type=F32)
            high, low = halves(jnp.concatenate([mid[:, :128], mid[:, 128:]], axis=0))
            expected = lax.dot_general(
                jnp.concatenate([high, low, high], axis=1),
                w3_ref[a],
                (((1,), (1,)), ((), ())),
                preferred_element_type=F32,
            )
            for k in range(2):
                util = (u_ref[a, 2 * n + k] + column_ref[a]) + row_ref[a, 0:1, :]
                score_ref[a, 2 * n + k] = util + DISCOUNT * expected[128 * k : 128 * k + 128]
        for k in range(2):
            scores = [score_ref[a, 2 * n + k] for a in range(4)]
            top = jnp.maximum(jnp.maximum(scores[0], scores[1]), jnp.maximum(scores[2], scores[3]))
            summed = sum(jnp.exp(s - top) for s in scores)
            lse_ref[n, k] = top + jnp.log(summed)

    def finish(n):
        swap(n).wait_recv()
        for k in range(2):
            ours, theirs = lse_ref[n, k], other_ref[n, k]
            top = jnp.maximum(ours, theirs)
            value = top + jnp.log(jnp.exp(ours - top) + jnp.exp(theirs - top))
            value_ref[2 * n + k] = value
            for a in range(4):
                prob_ref[a, 2 * n + k] = jnp.exp(score_ref[a, 2 * n + k] - value).astype(BF16)

    lax.fori_loop(0, 32, first_a, 0, unroll=4)
    second_a(0)
    send_a(0)
    lax.fori_loop(0, 8, first_b, 0)
    second_b(0)
    send_b(0)
    second_a(1)
    send_a(1)
    send_b(1)
    second_b(1)
    for c in (2, 3):
        send_a(c)
        send_b(c)
    for c in range(4):
        arrive(c)
        for n in (2 * c, 2 * c + 1):
            compute(n)
            if n > 0:
                swap(n - 1).start()
    swap(7).start()

    def stores(n):
        rows = pl.ds(2 * n, 2)
        return (
            pltpu.make_async_copy(value_ref.at[rows], value_out.at[rows], store_sem.at[0, n]),
            pltpu.make_async_copy(prob_ref.at[:, rows], prob_out.at[:, rows], store_sem.at[1, n]),
        )

    for n in range(8):
        finish(n)
        for copy in stores(n):
            copy.start()
    for c in range(4):
        settle(c, send_sem)
    for index, (ref, _, _) in enumerate(streams):
        part = ref.at[0, pl.ds(0, 31)]
        pltpu.make_async_copy(part, part, first_send.at[index]).wait()
    for copy in started:
        copy.wait_send()
    for n in range(8):
        swap(n).wait_send()
    for n in range(8):
        for copy in stores(n):
            copy.wait()


def whole(order, offsets, weights, first, second, third, fourth, v):
    dma = pltpu.SemaphoreType.DMA
    return pl.pallas_call(
        step_kernel,
        out_shape=(
            jax.ShapeDtypeStruct((16, 128, 128), F32),
            jax.ShapeDtypeStruct((4, 16, 128, 128), BF16),
        ),
        in_specs=[pl.BlockSpec(memory_space=pltpu.HBM)] * 8,
        out_specs=(pl.BlockSpec(memory_space=pltpu.HBM),) * 2,
        scratch_shapes=[
            pltpu.VMEM((16, 128, 128), F32),
            pltpu.VMEM((4, 16, 128, 128), BF16),
            dma((2, 8)),
            pltpu.SMEM((8,), jnp.int32),
            pltpu.SMEM((4, 8), jnp.int32),
            pltpu.SMEM((8, 64), F32),
            pltpu.SMEM((8, 64), F32),
            pltpu.VMEM((8, 4, 65), F32),
            pltpu.VMEM((8, 128), F32),
            pltpu.VMEM((8, 128), F32),
            pltpu.VMEM((2048, 128), F32),
            dma((8,)),
            pltpu.VMEM((2, 8, 64, 128), F32),
            pltpu.VMEM((2, 8, 64, 128), F32),
            pltpu.VMEM((4, 128, 384), BF16),
            pltpu.VMEM((4, 128, 384), BF16),
            pltpu.SMEM((4, 16), F32),
            pltpu.VMEM((4, 128, 128), F32),
            pltpu.VMEM((4, 8, 128), F32),
            pltpu.VMEM((8, 4, 256), F32),
            pltpu.VMEM((2, 32, 16, 128), F32),
            pltpu.VMEM((8, 32, 16, 128), F32),
            pltpu.VMEM((8, 32, 16, 128), F32),
            pltpu.VMEM((8, 512, 128), F32),
            pltpu.VMEM((4096, 128), F32),
            pltpu.VMEM((32, 2, 4, 16, 128), F32),
            pltpu.VMEM((8, 4, 2, 4, 16, 128), F32),
            pltpu.VMEM((4, 128, 16, 128), F32),
            pltpu.VMEM((4, 16, 128, 128), F32),
            pltpu.VMEM((8, 2, 128, 128), F32),
            pltpu.VMEM((8, 2, 128, 128), F32),
            dma((2,)),
            dma((2,)),
            dma((2,)),
            dma((2, 4, 2, 2)),
            dma((2, 4, 2, 2)),
            dma((2, 4)),
            dma((2, 4)),
            dma((2, 4)),
            dma((8,)),
            dma((8,)),
        ],
        compiler_params=pltpu.CompilerParams(collective_id=0, has_side_effects=True, vmem_limit_bytes=LIMIT),
        name="step",
    )(order, offsets.T, first, second, weights, third, fourth, v)


def body(
    value_now,
    cost_first,
    cost_second,
    cost_third,
    cost_fourth,
    trans_weights,
    trans_offsets,
    action_order,
):
    new_value, choice_prob = whole(
        action_order,
        trans_offsets,
        trans_weights,
        cost_first,
        cost_second,
        cost_third,
        cost_fourth,
        value_now.reshape(2048, 128),
    )
    return new_value.reshape(2, 8, 128, 128), choice_prob.reshape(4, 2, 8, 128, 128)


def solution(mesh):
    return jax.shard_map(
        body,
        mesh=mesh,
        in_specs=(P("wide", "narrow", None, None), P(), P(), P(), P(), P(), P(), P()),
        out_specs=(P("wide", "narrow", None, None), P("act", "wide", "narrow", None, None)),
        check_vma=False,
    )
```

```python
import jax
import jax.numpy as jnp
from jax import lax
from jax.experimental import pallas as pl
from jax.experimental.pallas import tpu as pltpu
from jax.sharding import PartitionSpec as P

DISCOUNT = 0.95
MESH = pl.DeviceIdType.MESH
F32 = jnp.float32
BF16 = jnp.bfloat16
VMEM = pl.BlockSpec(memory_space=pltpu.VMEM)
SMEM = pl.BlockSpec(memory_space=pltpu.SMEM)
LIMIT = 56 * 1024 * 1024


def place():
    wide = lax.axis_index("wide")
    return lax.div(wide, 4), lax.rem(wide, 4), lax.axis_index("narrow"), lax.axis_index("act")


def partner(step, t, q, sign):
    near = lax.rem(step, 8)
    far = lax.div(near + 1, 2)
    shift = sign * (1 - 2 * lax.rem(near + 1, 2)) * far
    mixed = lax.div(step, 8) + near
    return lax.rem(t + shift + 8, 8), mixed


def halves(x):
    high = x.astype(BF16)
    low = (x - high.astype(F32)).astype(BF16)
    return high, low


def builders(
    order_ref, offs_ref, first_ref, second_ref, w_ref, third_ref, fourth_ref,
    c0_ref, c1_ref, w2_ref, w3_ref, u_ref, column_ref, row_ref, pad_ref,
):
    act = lax.axis_index("act")
    first_row = lax.axis_index("wide") * 2
    second_row = lax.axis_index("narrow") * 8
    number = lax.broadcasted_iota(jnp.int32, (16, 256), 0)
    lane = lax.broadcasted_iota(jnp.int32, (16, 256), 1)
    zero = jnp.zeros((16, 256), F32)

    def prepare():
        pad_ref[...] = jnp.zeros_like(pad_ref)
        taps = w_ref[...]
        pad_ref[:, :, 0:65] = taps / jnp.sum(taps, axis=2, keepdims=True)

    def toeplitz(a, d, length, store):
        row = pad_ref[pl.ds(a, 1), d, :]
        shift = lax.rem(offs_ref[d, a] - 32 + 256, 256)
        base = pltpu.roll(jnp.broadcast_to(row, (16, 256)), shift, 1)
        for bit in (1, 2, 4, 8):
            base = jnp.where((number & bit) != 0, pltpu.roll(base, bit, 1), base)
        for start in range(0, length, 16):
            spread = pltpu.roll(base, start, 1) if start else base
            below = jnp.sum(jnp.where(lane >= 192, spread, zero), axis=1, keepdims=True)
            above = jnp.sum(jnp.where((lane >= length) & (lane < 192), spread, zero), axis=1, keepdims=True)
            full = jnp.where(lane == 0, spread + below, jnp.where(lane == length - 1, spread + above, spread))
            full = jnp.where(lane < length, full, zero)
            high = full.astype(BF16).astype(F32)
            store(pl.ds(start, 16), high, full - high)

    def outer(j, carry):
        a = order_ref[j]
        for d, ref in ((0, c0_ref), (1, c1_ref)):

            def store(rows, high, low):
                both = high + pltpu.roll(high, 64, 1) + pltpu.roll(low, 128, 1)
                ref[0, j, rows] = both[:, :128]
                ref[1, j, rows] = both[:, 128:]

            toeplitz(a, d, 64, store)
        return carry

    def inner(j, carry):
        a = order_ref[act * 4 + j]
        for d, ref in ((2, w2_ref), (3, w3_ref)):

            def store(rows, high, low):
                ref[j, rows, 0:128] = high[:, :128].astype(BF16)
                ref[j, rows, 128:256] = high[:, :128].astype(BF16)
                ref[j, rows, 256:384] = low[:, :128].astype(BF16)

            toeplitz(a, d, 128, store)
        column_ref[j] = jnp.broadcast_to(third_ref[pl.ds(a, 1), :], (128, 128)).T
        row_ref[j] = jnp.broadcast_to(fourth_ref[pl.ds(a, 1), :], (8, 128))
        for k in range(16):
            u_ref[j, k] = first_ref[a, first_row + k // 8] + second_ref[a, second_row + k % 8]
        return carry

    return prepare, outer, inner


def stack(x):
    high, low = halves(x)
    return jnp.concatenate([high, low, high, high], axis=0)


def wide_rows(ref, *index):
    return jnp.concatenate([ref[(half,) + index] for half in (0, 1)], axis=-1)


def step_kernel(
    order_in, offs_in, cost0_in, cost1_in, taps_in, cost2_in, cost3_in, v_in,
    value_out, prob_out,
    value_ref, prob_ref, store_sem,
    order_ref, offs_ref, cost0_ref, cost1_ref, taps_ref, cost2_ref, cost3_ref, v_ref, load_sem,
    c0_ref, c1_ref, w2_ref, w3_ref, u_ref, column_ref, row_ref, pad_ref,
    vt_ref, ga_ref, gb_ref, za_ref, zb_ref, ea_ref, eb_ref, r_ref, score_ref, lse_ref, other_ref,
    first_send, first_recv, first_local, ring_send, ring_recv,
    send_sem, recv_sem, local_sem, lse_send, lse_recv,
):
    y, q, z, act = place()
    wide = 4 * y + q
    row_a = y * 8 + q * 2 + act
    row_b = 64 + z * 8 + q * 2 + act
    barrier = pltpu.get_barrier_semaphore()
    loads = [
        pltpu.make_async_copy(src, dst, load_sem.at[n])
        for n, (src, dst) in enumerate(
            (
                (v_in, v_ref),
                (taps_in, taps_ref),
                (order_in, order_ref),
                (offs_in, offs_ref),
                (cost0_in, cost0_ref),
                (cost1_in, cost1_ref),
                (cost2_in, cost2_ref),
                (cost3_in, cost3_ref),
            )
        )
    ]
    for load in loads:
        load.start()
    prepare, build_outer, build_inner = builders(
        order_ref, offs_ref, cost0_ref, cost1_ref, taps_ref, cost2_ref, cost3_ref,
        c0_ref, c1_ref, w2_ref, w3_ref, u_ref, column_ref, row_ref, pad_ref,
    )

    def home_a(step):
        t, mixed = partner(step, y, q, 1)
        p = lax.rem(q + lax.rem(lax.div(mixed, 2), 4), 4)
        g = lax.rem(act + lax.rem(mixed, 2), 2)
        return ea_ref.at[4 * t + p, g], {"wide": 4 * t + p, "narrow": z, "act": g}

    def home_b(step):
        t, mixed = partner(step, z, q, -1)
        p = lax.rem(q + lax.rem(lax.div(mixed, 2), 4), 4)
        g = lax.rem(act + lax.rem(mixed, 2), 2)
        return eb_ref.at[t, p, g], {"wide": 4 * y + p, "narrow": t, "act": g}

    def greet(step, carry):
        pl.semaphore_signal(barrier, inc=1, device_id=home_a(step)[1], device_id_type=MESH)
        pl.semaphore_signal(barrier, inc=1, device_id=home_b(step)[1], device_id_type=MESH)
        return carry

    lax.fori_loop(1, 64, greet, 0, unroll=3)
    for load in loads:
        load.wait()

    def pick(n, carry):
        for half in (0, 1):
            vt_ref[half, n] = v_ref[pl.ds(64 * half + 2 * n + act, 16, stride=128), :]
        return carry

    lax.fori_loop(0, 32, pick, 0, unroll=4)
    prepare()
    pl.semaphore_wait(barrier, 126)

    def first(step, carry):
        t, mixed = partner(step, y, q, 1)
        p = lax.rem(q + lax.rem(mixed, 4), 4)
        pltpu.make_async_remote_copy(
            vt_ref.at[0, 4 * t + p],
            ga_ref.at[z, wide],
            first_send.at[0],
            first_recv.at[0],
            {"wide": 4 * t + p, "narrow": z, "act": act},
            MESH,
        ).start()
        t, mixed = partner(step, z, q, -1)
        p = lax.rem(q + lax.rem(mixed, 4), 4)
        pltpu.make_async_remote_copy(
            vt_ref.at[1, 4 * t + p],
            gb_ref.at[y, 4 * z + q],
            first_send.at[1],
            first_recv.at[1],
            {"wide": 4 * y + p, "narrow": t, "act": act},
            MESH,
        ).start()
        return carry

    lax.fori_loop(1, 32, first, 0, unroll=2)
    own = [
        pltpu.make_async_copy(vt_ref.at[0, wide], ga_ref.at[z, wide], first_local.at[0]),
        pltpu.make_async_copy(vt_ref.at[1, 4 * z + q], gb_ref.at[y, 4 * z + q], first_local.at[1]),
    ]
    for copy in own:
        copy.start()
    lax.fori_loop(0, 4, build_outer, 0, unroll=2)
    for copy in own:
        copy.wait()
    streams = (
        (ga_ref, z, lambda t: {"wide": wide, "narrow": t, "act": act}),
        (gb_ref, y, lambda t: {"wide": 4 * t + q, "narrow": z, "act": act}),
    )
    for index, (ref, _, _) in enumerate(streams):
        part = ref.at[0, pl.ds(0, 31)]
        pltpu.make_async_copy(part, part, first_recv.at[index]).wait()

    def hop(index, step, half, way):
        ref, t, device = streams[index]
        block = lax.rem(t + 8 - way * (step - 1), 8)
        piece = ref.at[block, pl.ds(16 * half, 16)]
        side = 0 if way > 0 else 1
        return pltpu.make_async_remote_copy(
            piece,
            piece,
            ring_send.at[index, step - 1, half, side],
            ring_recv.at[index, step - 1, half, side],
            device(lax.rem(t + 8 + way, 8)),
            MESH,
        )

    started = []
    for step in (1, 2, 3, 4):
        for half in (0, 1):
            for index in (0, 1):
                for way in (1, -1):
                    if step == 4 and half != (0 if way > 0 else 1):
                        continue
                    if step > 1:
                        hop(index, step - 1, half, way).wait_recv()
                    copy = hop(index, step, half, way)
                    copy.start()
                    started.append(copy)
        if step == 1:
            lax.fori_loop(4, 8, build_outer, 0, unroll=2)
        if step == 2:
            lax.fori_loop(0, 2, build_inner, 0, unroll=2)
        if step == 3:
            lax.fori_loop(2, 4, build_inner, 0, unroll=2)

    def gathered(index):
        hop(index, 3, 1, 1).wait_recv()
        hop(index, 3, 0, -1).wait_recv()
        hop(index, 4, 0, 1).wait_recv()
        hop(index, 4, 1, -1).wait_recv()

    def own_rows(ref, t):
        return wide_rows(ref, slice(None), pl.ds(t * 8, 8)).reshape(64, 256).astype(BF16)

    mine1 = own_rows(c1_ref, z)
    mine0 = own_rows(c0_ref, y)
    gb_rows = gb_ref.reshape(8, 512, 128)

    def first_a(w, carry):
        left = ga_ref[:, w, 0:8, :].reshape(64, 128)
        right = ga_ref[:, w, 8:16, :].reshape(64, 128)
        out = jnp.dot(mine1, stack(jnp.concatenate([left, right], axis=1)), preferred_element_type=F32)
        za_ref[:, pl.ds(16 * w, 8), :] = out[:, :128].reshape(8, 8, 128)
        za_ref[:, pl.ds(16 * w + 8, 8), :] = out[:, 128:].reshape(8, 8, 128)
        return carry


    def first_b(s, carry):
        for i in range(0, 8, 2):
            left = gb_rows[:, pl.ds(64 * s + i, 8, stride=8), :].reshape(64, 128)
            right = gb_rows[:, pl.ds(64 * s + i + 1, 8, stride=8), :].reshape(64, 128)
            out = jnp.dot(mine0, stack(jnp.concatenate([left, right], axis=1)), preferred_element_type=F32)
            zb_ref[pl.ds((8 * s + i) * 64, 64), :] = out[:, :128]
            zb_ref[pl.ds((8 * s + i + 1) * 64, 64), :] = out[:, 128:]
        return carry

    ea_rows = ea_ref.reshape(4096, 128)

    def second_a(part):
        def one(a, carry):
            left = jnp.concatenate([wide_rows(c0_ref, a, pl.ds(half, 32, stride=2)) for half in (0, 1)], axis=0)
            left = left.astype(BF16)
            for i in (0, 2):
                right = jnp.concatenate(
                    [za_ref[a, pl.ds(4 * part + i + k, 64, stride=8), :] for k in range(2)], axis=1
                )
                out = jnp.dot(left, stack(right), preferred_element_type=F32)
                for k in range(2):
                    for half in range(2):
                        start = lax.div(a, 4) * 64 + half * 32 + part * 16 + lax.rem(a, 4) * 4 + i + k
                        ea_rows[pl.ds(start, 32, stride=128), :] = out[
                            32 * half : 32 * half + 32, 128 * k : 128 * k + 128
                        ]
            return carry

        lax.fori_loop(0, 8, one, 0, unroll=2)

    def second_b(half):
        def one(g, carry):
            for a in range(4):
                left = wide_rows(c1_ref, 4 * g + a).astype(BF16)
                for p in (0, 2):
                    start = (4 * g + a) * 8 + 2 * p + half
                    right = jnp.concatenate(
                        [zb_ref[pl.ds(start + 2 * k, 64, stride=64), :] for k in range(2)], axis=1
                    )
                    out = jnp.dot(left, stack(right), preferred_element_type=F32)
                    for k in range(2):
                        block = out[:, 128 * k : 128 * k + 128].reshape(8, 8, 128)
                        for part in range(2):
                            eb_ref[:, p + k, g, 2 * half + part, 4 * a : 4 * a + 4, :] = block[
                                :, 4 * part : 4 * part + 4
                            ]
            return carry

        lax.fori_loop(0, 2, one, 0)

    groups = (pl.ds(0, 2), 2, 3)

    def local_a(m):
        c = groups[m]
        return pltpu.make_async_copy(ea_ref.at[wide, act, c], r_ref.at[c, row_a], local_sem.at[0, m])

    def local_b(m):
        c = groups[m]
        return pltpu.make_async_copy(eb_ref.at[z, q, act, c], r_ref.at[c, row_b], local_sem.at[1, m])

    def send_a(m):
        c = groups[m]
        local_a(m).start()

        def send(step, carry):
            src, device = home_a(step)
            pltpu.make_async_remote_copy(
                src.at[c], r_ref.at[c, row_a], send_sem.at[0, m], recv_sem.at[0, m], device, MESH
            ).start()
            return carry

        lax.fori_loop(1, 64, send, 0, unroll=3)

    def send_b(m):
        c = groups[m]
        local_b(m).start()

        def send(step, carry):
            src, device = home_b(step)
            pltpu.make_async_remote_copy(
                src.at[c], r_ref.at[c, row_b], send_sem.at[1, m], recv_sem.at[1, m], device, MESH
            ).start()
            return carry

        lax.fori_loop(1, 64, send, 0, unroll=3)

    def settle(m, sem):
        for index in (0, 1):
            part = r_ref.at[groups[m], pl.ds(0, 63)]
            pltpu.make_async_copy(part, part, sem.at[index, m]).wait()

    def arrive(m):
        local_a(m).wait()
        local_b(m).wait()
        settle(m, recv_sem)

    def swap(n):
        return pltpu.make_async_remote_copy(
            lse_ref.at[n], other_ref.at[n], lse_send.at[n], lse_recv.at[n], {"act": 1 - act}, MESH
        )

    def compute(n):
        flat = r_ref.at[n // 2].reshape(2048, 128)
        for a in range(4):
            rows = jnp.concatenate(
                [flat[pl.ds(4 * a + 2 * (n % 2) + k, 128, stride=16), :] for k in range(2)], axis=1
            )
            high, low = halves(rows)
            mid = jnp.dot(w2_ref[a], jnp.concatenate([high, low, high], axis=0), preferred_element_type=F32)
            high, low = halves(jnp.concatenate([mid[:, :128], mid[:, 128:]], axis=0))
            expected = lax.dot_general(
                jnp.concatenate([high, low, high], axis=1),
                w3_ref[a],
                (((1,), (1,)), ((), ())),
                preferred_element_type=F32,
            )
            for k in range(2):
                util = (u_ref[a, 2 * n + k] + column_ref[a]) + row_ref[a, 0:1, :]
                score_ref[a, 2 * n + k] = util + DISCOUNT * expected[128 * k : 128 * k + 128]
        for k in range(2):
            scores = [score_ref[a, 2 * n + k] for a in range(4)]
            top = jnp.maximum(jnp.maximum(scores[0], scores[1]), jnp.maximum(scores[2], scores[3]))
            summed = sum(jnp.exp(s - top) for s in scores)
            lse_ref[n, k] = top + jnp.log(summed)

    def finish(n):
        swap(n).wait_recv()
        for k in range(2):
            ours, theirs = lse_ref[n, k], other_ref[n, k]
            top = jnp.maximum(ours, theirs)
            value = top + jnp.log(jnp.exp(ours - top) + jnp.exp(theirs - top))
            value_ref[2 * n + k] = value
            for a in range(4):
                prob_ref[a, 2 * n + k] = jnp.exp(score_ref[a, 2 * n + k] - value).astype(BF16)

    gathered(1)
    lax.fori_loop(0, 8, first_b, 0)
    second_b(0)
    send_b(0)
    gathered(0)
    lax.fori_loop(0, 32, first_a, 0, unroll=4)
    second_a(0)
    second_a(1)
    send_a(0)
    second_b(1)
    for m in (1, 2):
        send_a(m)
        send_b(m)
    for m, pieces in enumerate(((0, 1, 2, 3), (4, 5), (6, 7))):
        arrive(m)
        for n in pieces:
            compute(n)
            if n > 0:
                swap(n - 1).start()
    swap(7).start()

    def stores(n):
        rows = pl.ds(2 * n, 2)
        return (
            pltpu.make_async_copy(value_ref.at[rows], value_out.at[rows], store_sem.at[0, n]),
            pltpu.make_async_copy(prob_ref.at[:, rows], prob_out.at[:, rows], store_sem.at[1, n]),
        )

    for n in range(8):
        finish(n)
        for copy in stores(n):
            copy.start()
    for m in range(3):
        settle(m, send_sem)
    for index, (ref, _, _) in enumerate(streams):
        part = ref.at[0, pl.ds(0, 31)]
        pltpu.make_async_copy(part, part, first_send.at[index]).wait()
    for copy in started:
        copy.wait_send()
    for n in range(8):
        swap(n).wait_send()
    for n in range(8):
        for copy in stores(n):
            copy.wait()


def whole(order, offsets, weights, first, second, third, fourth, v):
    dma = pltpu.SemaphoreType.DMA
    return pl.pallas_call(
        step_kernel,
        out_shape=(
            jax.ShapeDtypeStruct((16, 128, 128), F32),
            jax.ShapeDtypeStruct((4, 16, 128, 128), BF16),
        ),
        in_specs=[pl.BlockSpec(memory_space=pltpu.HBM)] * 8,
        out_specs=(pl.BlockSpec(memory_space=pltpu.HBM),) * 2,
        scratch_shapes=[
            pltpu.VMEM((16, 128, 128), F32),
            pltpu.VMEM((4, 16, 128, 128), BF16),
            dma((2, 8)),
            pltpu.SMEM((8,), jnp.int32),
            pltpu.SMEM((4, 8), jnp.int32),
            pltpu.SMEM((8, 64), F32),
            pltpu.SMEM((8, 64), F32),
            pltpu.VMEM((8, 4, 65), F32),
            pltpu.VMEM((8, 128), F32),
            pltpu.VMEM((8, 128), F32),
            pltpu.VMEM((2048, 128), F32),
            dma((8,)),
            pltpu.VMEM((2, 8, 64, 128), F32),
            pltpu.VMEM((2, 8, 64, 128), F32),
            pltpu.VMEM((4, 128, 384), BF16),
            pltpu.VMEM((4, 128, 384), BF16),
            pltpu.SMEM((4, 16), F32),
            pltpu.VMEM((4, 128, 128), F32),
            pltpu.VMEM((4, 8, 128), F32),
            pltpu.VMEM((8, 4, 256), F32),
            pltpu.VMEM((2, 32, 16, 128), F32),
            pltpu.VMEM((8, 32, 16, 128), F32),
            pltpu.VMEM((8, 32, 16, 128), F32),
            pltpu.VMEM((8, 512, 128), F32),
            pltpu.VMEM((4096, 128), F32),
            pltpu.VMEM((32, 2, 4, 16, 128), F32),
            pltpu.VMEM((8, 4, 2, 4, 16, 128), F32),
            pltpu.VMEM((4, 128, 16, 128), F32),
            pltpu.VMEM((4, 16, 128, 128), F32),
            pltpu.VMEM((8, 2, 128, 128), F32),
            pltpu.VMEM((8, 2, 128, 128), F32),
            dma((2,)),
            dma((2,)),
            dma((2,)),
            dma((2, 4, 2, 2)),
            dma((2, 4, 2, 2)),
            dma((2, 3)),
            dma((2, 3)),
            dma((2, 3)),
            dma((8,)),
            dma((8,)),
        ],
        compiler_params=pltpu.CompilerParams(collective_id=0, has_side_effects=True, vmem_limit_bytes=LIMIT),
        name="step",
    )(order, offsets.T, first, second, weights, third, fourth, v)


def body(
    value_now,
    cost_first,
    cost_second,
    cost_third,
    cost_fourth,
    trans_weights,
    trans_offsets,
    action_order,
):
    new_value, choice_prob = whole(
        action_order,
        trans_offsets,
        trans_weights,
        cost_first,
        cost_second,
        cost_third,
        cost_fourth,
        value_now.reshape(2048, 128),
    )
    return new_value.reshape(2, 8, 128, 128), choice_prob.reshape(4, 2, 8, 128, 128)


def solution(mesh):
    return jax.shard_map(
        body,
        mesh=mesh,
        in_specs=(P("wide", "narrow", None, None), P(), P(), P(), P(), P(), P(), P()),
        out_specs=(P("wide", "narrow", None, None), P("act", "wide", "narrow", None, None)),
        check_vma=False,
    )
```

```python
import jax
import jax.numpy as jnp
from jax import lax
from jax.experimental import pallas as pl
from jax.experimental.pallas import tpu as pltpu
from jax.sharding import PartitionSpec as P

DISCOUNT = 0.95
MESH = pl.DeviceIdType.MESH
F32 = jnp.float32
BF16 = jnp.bfloat16
VMEM = pl.BlockSpec(memory_space=pltpu.VMEM)
SMEM = pl.BlockSpec(memory_space=pltpu.SMEM)
LIMIT = 36 * 1024 * 1024


def place():
    wide = lax.axis_index("wide")
    return lax.div(wide, 4), lax.rem(wide, 4), lax.axis_index("narrow"), lax.axis_index("act")


def partner(step, t, q, sign):
    near = lax.rem(step, 8)
    far = lax.div(near + 1, 2)
    shift = sign * (1 - 2 * lax.rem(near + 1, 2)) * far
    mixed = lax.div(step, 8) + near
    return lax.rem(t + shift + 8, 8), mixed


def halves(x):
    high = x.astype(BF16)
    low = (x - high.astype(F32)).astype(BF16)
    return high, low


def builders(
    order_ref, offs_ref, first_ref, second_ref, w_ref, third_ref, fourth_ref,
    c0_ref, c1_ref, w2_ref, w3_ref, u_ref, column_ref, row_ref, pad_ref,
):
    act = lax.axis_index("act")
    first_row = lax.axis_index("wide") * 2
    second_row = lax.axis_index("narrow") * 8
    number = lax.broadcasted_iota(jnp.int32, (16, 256), 0)
    lane = lax.broadcasted_iota(jnp.int32, (16, 256), 1)
    zero = jnp.zeros((16, 256), F32)

    def prepare():
        pad_ref[...] = jnp.zeros_like(pad_ref)
        taps = w_ref[...]
        pad_ref[:, :, 0:65] = taps / jnp.sum(taps, axis=2, keepdims=True)

    def toeplitz(a, d, length, store):
        row = pad_ref[pl.ds(a, 1), d, :]
        shift = lax.rem(offs_ref[d, a] - 32 + 256, 256)
        base = pltpu.roll(jnp.broadcast_to(row, (16, 256)), shift, 1)
        for bit in (1, 2, 4, 8):
            base = jnp.where((number & bit) != 0, pltpu.roll(base, bit, 1), base)
        for start in range(0, length, 16):
            spread = pltpu.roll(base, start, 1) if start else base
            below = jnp.sum(jnp.where(lane >= 192, spread, zero), axis=1, keepdims=True)
            above = jnp.sum(jnp.where((lane >= length) & (lane < 192), spread, zero), axis=1, keepdims=True)
            full = jnp.where(lane == 0, spread + below, jnp.where(lane == length - 1, spread + above, spread))
            full = jnp.where(lane < length, full, zero)
            high = full.astype(BF16).astype(F32)
            store(pl.ds(start, 16), high, full - high)

    def outer(j, carry):
        a = order_ref[j]
        for d, ref in ((0, c0_ref), (1, c1_ref)):

            def store(rows, high, low):
                both = high + pltpu.roll(high, 64, 1) + pltpu.roll(low, 128, 1)
                ref[0, j, rows] = both[:, :128]
                ref[1, j, rows] = both[:, 128:]

            toeplitz(a, d, 64, store)
        return carry

    def inner(j, carry):
        a = order_ref[act * 4 + j]
        for d, ref in ((2, w2_ref), (3, w3_ref)):

            def store(rows, high, low):
                ref[j, rows, 0:128] = high[:, :128].astype(BF16)
                ref[j, rows, 128:256] = high[:, :128].astype(BF16)
                ref[j, rows, 256:384] = low[:, :128].astype(BF16)

            toeplitz(a, d, 128, store)
        column_ref[j] = jnp.broadcast_to(third_ref[pl.ds(a, 1), :], (128, 128)).T
        row_ref[j] = jnp.broadcast_to(fourth_ref[pl.ds(a, 1), :], (8, 128))
        for k in range(16):
            u_ref[j, k] = first_ref[a, first_row + k // 8] + second_ref[a, second_row + k % 8]
        return carry

    return prepare, outer, inner


def stack(x):
    high, low = halves(x)
    return jnp.concatenate([high, low, high, high], axis=0)


def wide_rows(ref, *index):
    return jnp.concatenate([ref[(half,) + index] for half in (0, 1)], axis=-1)


def step_kernel(
    order_in, offs_in, cost0_in, cost1_in, taps_in, cost2_in, cost3_in, v_in,
    value_out, prob_out,
    value_ref, prob_ref, store_sem,
    order_ref, offs_ref, cost0_ref, cost1_ref, taps_ref, cost2_ref, cost3_ref, v_ref, load_sem,
    c0_ref, c1_ref, w2_ref, w3_ref, u_ref, column_ref, row_ref, pad_ref,
    vt_ref, ga_ref, gb_ref, za_ref, zb_ref, ea_ref, eb_ref, r_ref, score_ref, lse_ref, other_ref,
    first_send, first_recv, first_local, ring_send, ring_recv,
    send_sem, recv_sem, local_sem, lse_send, lse_recv,
):
    y, q, z, act = place()
    wide = 4 * y + q
    row_a = y * 8 + q * 2 + act
    row_b = 64 + z * 8 + q * 2 + act
    barrier = pltpu.get_barrier_semaphore()
    loads = [
        pltpu.make_async_copy(src, dst, load_sem.at[n])
        for n, (src, dst) in enumerate(
            (
                (v_in, v_ref),
                (taps_in, taps_ref),
                (order_in, order_ref),
                (offs_in, offs_ref),
                (cost0_in, cost0_ref),
                (cost1_in, cost1_ref),
                (cost2_in, cost2_ref),
                (cost3_in, cost3_ref),
            )
        )
    ]
    for load in loads:
        load.start()
    prepare, build_outer, build_inner = builders(
        order_ref, offs_ref, cost0_ref, cost1_ref, taps_ref, cost2_ref, cost3_ref,
        c0_ref, c1_ref, w2_ref, w3_ref, u_ref, column_ref, row_ref, pad_ref,
    )

    def home_a(step):
        t, mixed = partner(step, y, q, 1)
        p = lax.rem(q + lax.rem(lax.div(mixed, 2), 4), 4)
        g = lax.rem(act + lax.rem(mixed, 2), 2)
        return ea_ref.at[4 * t + p, g], {"wide": 4 * t + p, "narrow": z, "act": g}

    def home_b(step):
        t, mixed = partner(step, z, q, -1)
        p = lax.rem(q + lax.rem(lax.div(mixed, 2), 4), 4)
        g = lax.rem(act + lax.rem(mixed, 2), 2)
        return eb_ref.at[t, p, g], {"wide": 4 * y + p, "narrow": t, "act": g}

    def greet(step, carry):
        pl.semaphore_signal(barrier, inc=1, device_id=home_a(step)[1], device_id_type=MESH)
        pl.semaphore_signal(barrier, inc=1, device_id=home_b(step)[1], device_id_type=MESH)
        return carry

    lax.fori_loop(1, 64, greet, 0, unroll=3)
    for load in loads:
        load.wait()

    def pick(n, carry):
        for half in (0, 1):
            vt_ref[half, n] = v_ref[pl.ds(64 * half + 2 * n + act, 16, stride=128), :]
        return carry

    lax.fori_loop(0, 32, pick, 0, unroll=4)
    prepare()
    pl.semaphore_wait(barrier, 126)

    def first(step, carry):
        t, mixed = partner(step, y, q, 1)
        p = lax.rem(q + lax.rem(mixed, 4), 4)
        pltpu.make_async_remote_copy(
            vt_ref.at[0, 4 * t + p],
            ga_ref.at[z, wide],
            first_send.at[0],
            first_recv.at[0],
            {"wide": 4 * t + p, "narrow": z, "act": act},
            MESH,
        ).start()
        t, mixed = partner(step, z, q, -1)
        p = lax.rem(q + lax.rem(mixed, 4), 4)
        pltpu.make_async_remote_copy(
            vt_ref.at[1, 4 * t + p],
            gb_ref.at[y, 4 * z + q],
            first_send.at[1],
            first_recv.at[1],
            {"wide": 4 * y + p, "narrow": t, "act": act},
            MESH,
        ).start()
        return carry

    lax.fori_loop(1, 32, first, 0, unroll=2)
    own = [
        pltpu.make_async_copy(vt_ref.at[0, wide], ga_ref.at[z, wide], first_local.at[0]),
        pltpu.make_async_copy(vt_ref.at[1, 4 * z + q], gb_ref.at[y, 4 * z + q], first_local.at[1]),
    ]
    for copy in own:
        copy.start()
    lax.fori_loop(0, 4, build_outer, 0, unroll=2)
    for copy in own:
        copy.wait()
    streams = (
        (ga_ref, z, lambda t: {"wide": wide, "narrow": t, "act": act}),
        (gb_ref, y, lambda t: {"wide": 4 * t + q, "narrow": z, "act": act}),
    )
    for index, (ref, _, _) in enumerate(streams):
        part = ref.at[0, pl.ds(0, 31)]
        pltpu.make_async_copy(part, part, first_recv.at[index]).wait()

    def hop(index, step, half, way):
        ref, t, device = streams[index]
        block = lax.rem(t + 8 - way * (step - 1), 8)
        piece = ref.at[block, pl.ds(16 * half, 16)]
        side = 0 if way > 0 else 1
        return pltpu.make_async_remote_copy(
            piece,
            piece,
            ring_send.at[index, step - 1, half, side],
            ring_recv.at[index, step - 1, half, side],
            device(lax.rem(t + 8 + way, 8)),
            MESH,
        )

    started = []
    for step in (1, 2, 3, 4):
        for half in (0, 1):
            for index in (0, 1):
                for way in (1, -1):
                    if step == 4 and half != (0 if way > 0 else 1):
                        continue
                    if step > 1:
                        hop(index, step - 1, half, way).wait_recv()
                    copy = hop(index, step, half, way)
                    copy.start()
                    started.append(copy)
        if step == 1:
            lax.fori_loop(4, 8, build_outer, 0, unroll=2)
        if step == 2:
            lax.fori_loop(0, 2, build_inner, 0, unroll=2)
        if step == 3:
            lax.fori_loop(2, 4, build_inner, 0, unroll=2)

    def gathered(index):
        hop(index, 3, 1, 1).wait_recv()
        hop(index, 3, 0, -1).wait_recv()
        hop(index, 4, 0, 1).wait_recv()
        hop(index, 4, 1, -1).wait_recv()

    def own_rows(ref, t):
        return wide_rows(ref, slice(None), pl.ds(t * 8, 8)).reshape(64, 256).astype(BF16)

    mine1 = own_rows(c1_ref, z)
    mine0 = own_rows(c0_ref, y)
    gb_rows = gb_ref.reshape(8, 512, 128)

    def first_a(w, carry):
        left = ga_ref[:, w, 0:8, :].reshape(64, 128)
        right = ga_ref[:, w, 8:16, :].reshape(64, 128)
        out = jnp.dot(mine1, stack(jnp.concatenate([left, right], axis=1)), preferred_element_type=F32)
        za_ref[:, pl.ds(16 * w, 8), :] = out[:, :128].reshape(8, 8, 128)
        za_ref[:, pl.ds(16 * w + 8, 8), :] = out[:, 128:].reshape(8, 8, 128)
        return carry


    def first_b(s, carry):
        for i in range(0, 8, 2):
            left = gb_rows[:, pl.ds(64 * s + i, 8, stride=8), :].reshape(64, 128)
            right = gb_rows[:, pl.ds(64 * s + i + 1, 8, stride=8), :].reshape(64, 128)
            out = jnp.dot(mine0, stack(jnp.concatenate([left, right], axis=1)), preferred_element_type=F32)
            zb_ref[pl.ds((8 * s + i) * 64, 64), :] = out[:, :128]
            zb_ref[pl.ds((8 * s + i + 1) * 64, 64), :] = out[:, 128:]
        return carry

    ea_rows = ea_ref.reshape(4096, 128)

    def second_a(part):
        def one(a, carry):
            left = jnp.concatenate([wide_rows(c0_ref, a, pl.ds(half, 32, stride=2)) for half in (0, 1)], axis=0)
            left = left.astype(BF16)
            for i in (0, 2):
                right = jnp.concatenate(
                    [za_ref[a, pl.ds(4 * part + i + k, 64, stride=8), :] for k in range(2)], axis=1
                )
                out = jnp.dot(left, stack(right), preferred_element_type=F32)
                for k in range(2):
                    for half in range(2):
                        start = lax.div(a, 4) * 64 + half * 32 + part * 16 + lax.rem(a, 4) * 4 + i + k
                        ea_rows[pl.ds(start, 32, stride=128), :] = out[
                            32 * half : 32 * half + 32, 128 * k : 128 * k + 128
                        ]
            return carry

        lax.fori_loop(0, 8, one, 0, unroll=2)

    def second_b(half):
        def one(g, carry):
            for a in range(4):
                left = wide_rows(c1_ref, 4 * g + a).astype(BF16)
                for p in (0, 2):
                    start = (4 * g + a) * 8 + 2 * p + half
                    right = jnp.concatenate(
                        [zb_ref[pl.ds(start + 2 * k, 64, stride=64), :] for k in range(2)], axis=1
                    )
                    out = jnp.dot(left, stack(right), preferred_element_type=F32)
                    for k in range(2):
                        block = out[:, 128 * k : 128 * k + 128].reshape(8, 8, 128)
                        for part in range(2):
                            eb_ref[:, p + k, g, 2 * half + part, 4 * a : 4 * a + 4, :] = block[
                                :, 4 * part : 4 * part + 4
                            ]
            return carry

        lax.fori_loop(0, 2, one, 0)

    groups = (pl.ds(0, 2), 2, 3)

    def local_a(m):
        c = groups[m]
        return pltpu.make_async_copy(ea_ref.at[wide, act, c], r_ref.at[c, row_a], local_sem.at[0, m])

    def local_b(m):
        c = groups[m]
        return pltpu.make_async_copy(eb_ref.at[z, q, act, c], r_ref.at[c, row_b], local_sem.at[1, m])

    def send_a(m):
        c = groups[m]
        local_a(m).start()

        def send(step, carry):
            src, device = home_a(step)
            pltpu.make_async_remote_copy(
                src.at[c], r_ref.at[c, row_a], send_sem.at[0, m], recv_sem.at[0, m], device, MESH
            ).start()
            return carry

        lax.fori_loop(1, 64, send, 0, unroll=3)

    def send_b(m):
        c = groups[m]
        local_b(m).start()

        def send(step, carry):
            src, device = home_b(step)
            pltpu.make_async_remote_copy(
                src.at[c], r_ref.at[c, row_b], send_sem.at[1, m], recv_sem.at[1, m], device, MESH
            ).start()
            return carry

        lax.fori_loop(1, 64, send, 0, unroll=3)

    def settle(m, sem):
        for index in (0, 1):
            part = r_ref.at[groups[m], pl.ds(0, 63)]
            pltpu.make_async_copy(part, part, sem.at[index, m]).wait()

    def arrive(m):
        local_a(m).wait()
        local_b(m).wait()
        settle(m, recv_sem)

    def swap(n):
        return pltpu.make_async_remote_copy(
            lse_ref.at[n], other_ref.at[n], lse_send.at[n], lse_recv.at[n], {"act": 1 - act}, MESH
        )

    def compute(n, between=None):
        flat = r_ref.at[n // 2].reshape(2048, 128)
        for a in range(4):
            rows = jnp.concatenate(
                [flat[pl.ds(4 * a + 2 * (n % 2) + k, 128, stride=16), :] for k in range(2)], axis=1
            )
            high, low = halves(rows)
            mid = jnp.dot(w2_ref[a], jnp.concatenate([high, low, high], axis=0), preferred_element_type=F32)
            high, low = halves(jnp.concatenate([mid[:, :128], mid[:, 128:]], axis=0))
            expected = lax.dot_general(
                jnp.concatenate([high, low, high], axis=1),
                w3_ref[a],
                (((1,), (1,)), ((), ())),
                preferred_element_type=F32,
            )
            for k in range(2):
                util = (u_ref[a, 2 * n + k] + column_ref[a]) + row_ref[a, 0:1, :]
                score_ref[a, 2 * n + k] = util + DISCOUNT * expected[128 * k : 128 * k + 128]
            if a == 0 and between is not None:
                between()
        for k in range(2):
            scores = [score_ref[a, 2 * n + k] for a in range(4)]
            top = jnp.maximum(jnp.maximum(scores[0], scores[1]), jnp.maximum(scores[2], scores[3]))
            summed = sum(jnp.exp(s - top) for s in scores)
            lse_ref[n, k] = top + jnp.log(summed)

    def finish(n):
        swap(n).wait_recv()
        for k in range(2):
            ours, theirs = lse_ref[n, k], other_ref[n, k]
            top = jnp.maximum(ours, theirs)
            value = top + jnp.log(jnp.exp(ours - top) + jnp.exp(theirs - top))
            value_ref[2 * n + k] = value
            for a in range(4):
                prob_ref[a, 2 * n + k] = jnp.exp(score_ref[a, 2 * n + k] - value).astype(BF16)

    gathered(1)
    lax.fori_loop(0, 8, first_b, 0)
    second_b(0)
    send_b(0)
    gathered(0)
    lax.fori_loop(0, 32, first_a, 0, unroll=4)
    second_a(0)
    second_a(1)
    send_a(0)
    second_b(1)
    for m in (1, 2):
        send_a(m)
        send_b(m)
    for m, pieces in enumerate(((0, 1, 2, 3), (4, 5), (6, 7))):
        arrive(m)
        for n in pieces:
            compute(n, swap(n - 1).start if n > 0 else None)
    swap(7).start()

    def stores(n):
        rows = pl.ds(2 * n, 2)
        return (
            pltpu.make_async_copy(value_ref.at[rows], value_out.at[rows], store_sem.at[0, n]),
            pltpu.make_async_copy(prob_ref.at[:, rows], prob_out.at[:, rows], store_sem.at[1, n]),
        )

    for n in range(8):
        finish(n)
        for copy in stores(n):
            copy.start()
    for m in range(3):
        settle(m, send_sem)
    for index, (ref, _, _) in enumerate(streams):
        part = ref.at[0, pl.ds(0, 31)]
        pltpu.make_async_copy(part, part, first_send.at[index]).wait()
    for copy in started:
        copy.wait_send()
    for n in range(8):
        swap(n).wait_send()
    for n in range(8):
        for copy in stores(n):
            copy.wait()


def whole(order, offsets, weights, first, second, third, fourth, v):
    dma = pltpu.SemaphoreType.DMA
    operands = (order, offsets.T, first, second, weights, third, fourth, v)
    return pl.pallas_call(
        step_kernel,
        out_shape=(
            jax.ShapeDtypeStruct((16, 128, 128), F32),
            jax.ShapeDtypeStruct((4, 16, 128, 128), BF16),
        ),
        in_specs=[pl.BlockSpec(memory_space=pltpu.HBM)] * 8,
        out_specs=(pl.BlockSpec(memory_space=pl.ANY),) * 2,
        scratch_shapes=[
            pltpu.VMEM((16, 128, 128), F32),
            pltpu.VMEM((4, 16, 128, 128), BF16),
            dma((2, 8)),
            pltpu.SMEM((8,), jnp.int32),
            pltpu.SMEM((4, 8), jnp.int32),
            pltpu.SMEM((8, 64), F32),
            pltpu.SMEM((8, 64), F32),
            pltpu.VMEM((8, 4, 65), F32),
            pltpu.VMEM((8, 128), F32),
            pltpu.VMEM((8, 128), F32),
            pltpu.VMEM((2048, 128), F32),
            dma((8,)),
            pltpu.VMEM((2, 8, 64, 128), F32),
            pltpu.VMEM((2, 8, 64, 128), F32),
            pltpu.VMEM((4, 128, 384), BF16),
            pltpu.VMEM((4, 128, 384), BF16),
            pltpu.SMEM((4, 16), F32),
            pltpu.VMEM((4, 128, 128), F32),
            pltpu.VMEM((4, 8, 128), F32),
            pltpu.VMEM((8, 4, 256), F32),
            pltpu.VMEM((2, 32, 16, 128), F32),
            pltpu.VMEM((8, 32, 16, 128), F32),
            pltpu.VMEM((8, 32, 16, 128), F32),
            pltpu.VMEM((8, 512, 128), F32),
            pltpu.VMEM((4096, 128), F32),
            pltpu.VMEM((32, 2, 4, 16, 128), F32),
            pltpu.VMEM((8, 4, 2, 4, 16, 128), F32),
            pltpu.VMEM((4, 128, 16, 128), F32),
            pltpu.VMEM((4, 16, 128, 128), F32),
            pltpu.VMEM((8, 2, 128, 128), F32),
            pltpu.VMEM((8, 2, 128, 128), F32),
            dma((2,)),
            dma((2,)),
            dma((2,)),
            dma((2, 4, 2, 2)),
            dma((2, 4, 2, 2)),
            dma((2, 3)),
            dma((2, 3)),
            dma((2, 3)),
            dma((8,)),
            dma((8,)),
        ],
        compiler_params=pltpu.CompilerParams(collective_id=0, has_side_effects=True, vmem_limit_bytes=LIMIT),
        name="step",
    )(*(pltpu.with_memory_space_constraint(x, pltpu.HBM) for x in operands))


def body(
    value_now,
    cost_first,
    cost_second,
    cost_third,
    cost_fourth,
    trans_weights,
    trans_offsets,
    action_order,
):
    new_value, choice_prob = whole(
        action_order,
        trans_offsets,
        trans_weights,
        cost_first,
        cost_second,
        cost_third,
        cost_fourth,
        value_now.reshape(2048, 128),
    )
    return new_value.reshape(2, 8, 128, 128), choice_prob.reshape(4, 2, 8, 128, 128)


def solution(mesh):
    return jax.shard_map(
        body,
        mesh=mesh,
        in_specs=(P("wide", "narrow", None, None), P(), P(), P(), P(), P(), P(), P()),
        out_specs=(P("wide", "narrow", None, None), P("act", "wide", "narrow", None, None)),
        check_vma=False,
    )
```
